32 devices in a mesh: dp: 4 (over y, x), mp: 8 (over z, core).
Axes of the slice: x: 2, y: 2, z: 4, core: 2. Of those that a mesh axis runs over, the one named last changes fastest.
Arguments:
- features: bfloat16 [1536, 8192], P('dp', 'mp'), may hold values from -6 to 6
- cotangent: bfloat16 [1536, 8192], P('dp', 'mp'), may hold values from -6 to 6
- weights: bfloat16 [2, 8192, 8192], P(None, 'mp'), may hold values from -0.0625 to 0.0625
- biases: float32 [2, 8192], P(None, 'mp'), may hold values from -3 to 3
- weight_accum: float32 [2, 8192], P(None, ('mp', 'dp')), may hold values from 100 to 16000
- owner_slot: int32 [128], replicated, may hold values from 0 to 127, each once
- bag_ids: int32 [128, 1536, 4], P(('dp', 'mp')), may hold values from 0 to 8191
- bag_length: int32 [128, 1536], P(('dp', 'mp')), may hold values from 1 to 4, as said below
- tables: float32 [128, 8192, 64], P(('dp', 'mp')), may hold values from -3 to 3
- table_accum: float32 [128, 8192], P(('dp', 'mp')), may hold values from 1 to 256
Outputs:
- weight_step: float32 [2, 8192, 8192], P(None, ('mp', 'dp'))
- new_weight_accum: float32 [2, 8192], P(None, ('mp', 'dp'))
- new_tables: float32 [128, 8192, 64], P(('dp', 'mp'))
- new_table_accum: float32 [128, 8192], P(('dp', 'mp'))
The draws below stay inside these ranges and needn't reach their ends.
Inputs may be any that keep to these rules, and one draw needn't show every extreme that they name: `owner_slot`: A permutation; the owner slot s lies on device s // 4 in the order of dp+mp, as its entry s % 4. Only the first bag_length ids of a bag are looked up.
All inputs are finite; a program needn't handle non-finite values.
Results may differ from the reference program's by a relative error of at most 0.025.
Values may be sent and summed in bfloat16 or wider, within the bound.
No kernel may reach another device: no remote copies, remote signals or barrier semaphores. Data moves between devices by JAX's collectives and lax.ppermute only.
A program may use at most 192 MiB of HBM per device.

```python
import math
import jax
import jax.numpy as jnp
import numpy as np
from jax import lax

F = 128
E = 64
D = 8192
ROWS_DEV = 384
BATCH = 1536
LAYERS = 2
BAG = 4
VOCAB = 8192
N_DP = 4
N_MP = 8


def draw_bag_length(key, part):
    lengths = jax.random.randint(key, (F, BATCH), 1, BAG + 1)
    lengths = lengths.at[0, 0].set(BAG).at[0, 1].set(1)
    return lengths.astype(jnp.int32)


def touch_ends(array, rng, least, top_value):
    dims = array.shape
    spot = [jax.random.randint(jax.random.fold_in(rng, axis), (), 0, dims[axis]) for axis in range(len(dims))]
    array = array.at[tuple(spot)].set(least)
    longest = dims.index(max(dims))
    spot[longest] = (spot[longest] + 1) % dims[longest]
    return array.at[tuple(spot)].set(top_value)


def with_spikes(values, own_key, source, target, shards_of, factor):
    def block_of(axis_at):
        return (jnp.arange(values.shape[axis_at]) // (values.shape[axis_at] // shards_of)).reshape((-1,) + (1,) * (values.ndim - 1 - axis_at))

    near = jax.random.permutation(own_key, shards_of)[block_of(target)]
    second = (block_of(target) + shards_of // 2) % shards_of
    return jnp.where((block_of(source) == near) | (block_of(source) == second), factor * values, values)


def level_of(own_key, dims, pieces, smallest, high):
    loudness, own = 1.0, jax.random.fold_in(own_key, 6)
    for position, blocks in pieces:
        steps = jnp.exp(jax.random.uniform(jax.random.fold_in(own, position), (blocks,), jnp.float32, smallest / len(pieces), high / len(pieces)))
        loudness = loudness * jnp.repeat(steps, dims[position] // blocks).reshape([-1 if axis == position else 1 for axis in range(len(dims))])
    return loudness


def rank_table(amount, skew):
    loads = [(1 << 20) // math.isqrt(rank ** skew) + 1 for rank in range(1, amount + 1)]
    scale = 1 + sum(loads) // (1 << 30)
    return np.cumsum(np.array([max(1, weight // scale) for weight in loads]))


def skewed_ids(rng, dims, amount, skew):
    listing = rank_table(amount, skew)
    ticket = jax.random.randint(jax.random.fold_in(rng, 1), dims, 0, int(listing[amount - 1]))
    grade = jnp.searchsorted(jnp.asarray(listing, jnp.int32), ticket, side="right")
    return jax.random.permutation(jax.random.fold_in(rng, 2), amount)[grade].astype(jnp.int32)


def scatter_about(stream_key, extent, scale, bound, split=(), kind=jnp.bfloat16):
    drawn = jax.random.normal(stream_key, extent, jnp.float32) * scale
    if len(split) > 0:
        drawn = level_of(stream_key, extent, split, -0.22, 0.18) * drawn
    return jnp.clip(drawn, min=-bound, max=bound).astype(kind)


def gaussian_with(key, shape, deviation, reach, shards, heavy, kind=jnp.bfloat16):
    drawn = deviation * jax.random.normal(key, shape, jnp.float32)
    if shards:
        drawn = drawn * level_of(key, shape, shards, -0.22, 0.18)
    return jnp.clip(with_spikes(drawn, jax.random.fold_in(key, 3), *heavy), -reach, reach).astype(kind)


def setup_inputs(seed: int = 0) -> dict:
    streams_of = jax.random.split(jax.random.key(seed), 11)
    return {
        "features": scatter_about(streams_of[0], (BATCH, D), 1.0, 6.0, ((0, 4), (1, 8))),
        "cotangent": gaussian_with(streams_of[1], (BATCH, D), 1.0, 6.0, ((0, 4), (1, 8)), (0, 1, 8, 2.0)),
        "weights": scatter_about(streams_of[2], (LAYERS, D, D), D ** -0.5, 0.0625, ((1, 8),)),
        "biases": scatter_about(streams_of[3], (LAYERS, D), 0.5, 3.0, ((1, 8),), jnp.float32),
        "weight_accum": jnp.clip(jnp.exp(math.log(16000.0) - 5.075174 * jax.random.uniform(streams_of[4], (LAYERS, D), jnp.float32) ** level_of(streams_of[4], (LAYERS, D), ((1, 32),), -0.2, 0.2)), 100.0, 16000.0),
        "owner_slot": jax.random.permutation(streams_of[5], F).astype(jnp.int32),
        "bag_ids": touch_ends(skewed_ids(streams_of[6], (F, BATCH, BAG), VOCAB, 2), jax.random.fold_in(streams_of[6], 3), 0, VOCAB - 1).astype(jnp.int32),
        "bag_length": draw_bag_length(jax.random.fold_in(streams_of[10], 71), 0),
        "tables": scatter_about(streams_of[8], (F, VOCAB, E), 0.5, 3.0, ((0, 32),), jnp.float32),
        "table_accum": jnp.clip(jnp.exp(math.log(256.0) - 5.5451774 * jax.random.uniform(streams_of[9], (F, VOCAB), jnp.float32) ** level_of(streams_of[9], (F, VOCAB), ((0, 32),), -0.2, 0.2)), 1.0, 256.0),
    }


learn_rate = 0.5

def rounded(values):
    return lax.optimization_barrier(values.astype(jnp.bfloat16)).astype(jnp.float32)

def block_sum(scaled, weight, added):
    width = D // N_MP
    summed = jnp.zeros((scaled.shape[0], D), jnp.float32)
    for part_idx in range(N_MP):
        first = part_idx * width
        partial_value = jnp.dot(scaled[:, first:first + width], weight[first:first + width, :], preferred_element_type=jnp.float32)
        if added is not None:
            partial_value = partial_value.at[:, first:first + width].add(added[:, first:first + width])
        summed = summed + rounded(partial_value)
    return summed

def update_rows(grads, row_ids, length, table, accum):
    in_bag = jnp.arange(row_ids.shape[1], dtype=jnp.int32)[None, :] < length[:, None]
    spread = jnp.where(in_bag[:, :, None], grads.astype(jnp.float32)[:, None, :], jnp.float32(0.0))
    summed = jax.ops.segment_sum(spread.reshape(-1, grads.shape[1]), row_ids.reshape(-1), num_segments=table.shape[0])
    renewed = accum + lax.optimization_barrier(jnp.mean(summed * summed, axis=1))
    return (table - learn_rate * summed / jnp.sqrt(renewed)[:, None], renewed)

def reference(features, cotangent, weights, biases, weight_accum, owner_slot, bag_ids, bag_length, tables, table_accum):
    base_f32 = features.astype(jnp.float32)
    current = features
    layer_inputs = []
    preacts = []
    for layer_idx in range(LAYERS):
        preact = lax.dot_general(current, weights[layer_idx], (((1,), (1,)), ((), ())), preferred_element_type=jnp.float32) + biases[layer_idx]
        layer_inputs.append(current)
        preacts.append(preact)
        current = (base_f32 * preact + current.astype(jnp.float32)).astype(jnp.bfloat16)
    upstream = cotangent.astype(jnp.float32)
    carried = jnp.zeros_like(upstream)
    updates = [None] * LAYERS
    accums = [None] * LAYERS
    pooled = None
    for layer_idx in range(LAYERS - 1, -1, -1):
        scaled = (upstream * base_f32).astype(jnp.bfloat16)
        carried = carried + upstream * preacts[layer_idx]
        weight_grad = jnp.zeros((D, D), jnp.float32)
        for group in range(N_DP):
            first = group * ROWS_DEV
            product = lax.dot_general(scaled[first:first + ROWS_DEV], layer_inputs[layer_idx][first:first + ROWS_DEV], (((0,), (0,)), ((), ())), preferred_element_type=jnp.float32)
            weight_grad = weight_grad + rounded(product)
        renewed = weight_accum[layer_idx] + lax.optimization_barrier(jnp.mean(weight_grad * weight_grad, axis=1))
        updates[layer_idx] = weight_grad / jnp.sqrt(renewed)[:, None]
        accums[layer_idx] = renewed
        if layer_idx > 0:
            upstream = upstream + block_sum(scaled, weights[layer_idx], None)
        else:
            pooled = block_sum(scaled, weights[0], upstream + carried).astype(jnp.bfloat16)
    blocks = pooled.reshape(BATCH, F, E)
    inverse = jnp.zeros((F,), jnp.int32).at[owner_slot].set(jnp.arange(F, dtype=jnp.int32))
    slotted = jnp.take(blocks, inverse, axis=1)
    new_tables, new_accum = jax.vmap(update_rows, in_axes=(1, 0, 0, 0, 0))(slotted, bag_ids, bag_length, tables, table_accum)
    return (jnp.stack(updates), jnp.stack(accums), new_tables, new_accum)
```

```python
import functools
import jax, jax.numpy as jnp
from jax import lax
from jax.experimental import pallas as pl
from jax.experimental.pallas import tpu as pltpu
from jax.sharding import PartitionSpec as P


learn_rate = 0.5
cores = 2


def embed_kernel(n_tab, bag, batch, embed, chunk, unroll, rate, ids_ref, g_ref, tab_ref, acc_in_ref, tab_out, acc_out, rows, *accs):
    step = pl.program_id(0)
    pairs = g_ref.shape[1]

    @pl.when(step == 0)
    def _():
        src, _, per, lanes = g_ref.shape
        for a in accs:
            a[...] = jnp.zeros_like(a)
        for p in range(pairs):
            rows[p] = g_ref[:, p].astype(jnp.float32).reshape(src * per, lanes)

        def one(i, carry):
            for u in range(unroll):
                b = i * unroll + u
                vals = [rows[p, pl.ds(b, 1), :] for p in range(pairs)]
                for j in range(bag):
                    for t in range(n_tab):
                        v = ids_ref[(t * bag + j) * batch + b]
                        accs[t][pl.ds(v, 1), :] += vals[t // 2]
            return carry

        lax.fori_loop(0, batch // unroll, one, 0)

    base = pl.multiple_of(step * chunk, chunk)
    for p in range(pairs):
        first = accs[2 * p][pl.ds(base, chunk), :]
        if 2 * p + 1 < n_tab:
            second = accs[2 * p + 1][pl.ds(base, chunk), :]
            lane = lax.broadcasted_iota(jnp.int32, first.shape, 1)
            first = jnp.where(lane < embed, first, second)
        turned = first.T
        for o in range(min(2, n_tab - 2 * p)):
            t = 2 * p + o
            grad = turned[o * embed:(o + 1) * embed, :]
            renewed = acc_in_ref[t:t + 1, :] + jnp.sum(grad * grad, axis=0, keepdims=True) * (1.0 / embed)
            acc_out[t:t + 1, :] = renewed
            tab_out[t] = tab_ref[t] - (rate * grad) / jnp.sqrt(renewed)


def embed_update(ids, grads, tables_t, accum, bag, batch, rate, chunk=1024, unroll=8):
    n_tab, embed, vocab = tables_t.shape
    chunk = min(chunk, vocab)
    kern = functools.partial(embed_kernel, n_tab, bag, batch, embed, chunk, unroll, rate)
    return pl.pallas_call(
        kern,
        out_shape=(jax.ShapeDtypeStruct(tables_t.shape, jnp.float32), jax.ShapeDtypeStruct(accum.shape, jnp.float32)),
        grid_spec=pltpu.PrefetchScalarGridSpec(
            num_scalar_prefetch=1,
            grid=(vocab // chunk,),
            in_specs=[
                pl.BlockSpec(grads.shape, lambda i, s: (0,) * 4, pipeline_mode=pl.Buffered(1)),
                pl.BlockSpec((n_tab, embed, chunk), lambda i, s: (0, 0, i)),
                pl.BlockSpec((n_tab, chunk), lambda i, s: (0, i)),
            ],
            out_specs=[
                pl.BlockSpec((n_tab, embed, chunk), lambda i, s: (0, 0, i)),
                pl.BlockSpec((n_tab, chunk), lambda i, s: (0, i)),
            ],
            scratch_shapes=[pltpu.VMEM((grads.shape[1], batch, grads.shape[3]), jnp.float32)]
            + [pltpu.VMEM((vocab + 8, grads.shape[3]), jnp.float32) for _ in range(n_tab)],
        ),
        compiler_params=pltpu.CompilerParams(dimension_semantics=("arbitrary",), vmem_limit_bytes=56 * 1024 * 1024),
        cost_estimate=pl.CostEstimate(flops=100000000, bytes_accessed=150000000, transcendentals=0),
        name="embed_update",
    )(ids, grads, tables_t, accum)


def tile_of(size, limit):
    return max(t for t in range(128, limit + 1, 128) if size % t == 0)


def turn_kernel(parts, index_ref, value_ref, turned_ref, own_ref, other_ref):
    share = own_ref.shape[1]
    width = value_ref.shape[1]
    for first in range(0, width, 128):
        turned_ref[first : first + 128, :] = value_ref[:, first : first + 128].T
    for which, out in enumerate((own_ref, other_ref)):
        for k in range(parts):
            start = pl.multiple_of(index_ref[which * parts + k] * share, share)
            out[k] = turned_ref[pl.ds(start, share), :]


def turn(sent_index, value, parts, share):
    rows, width = value.shape
    return pl.pallas_call(
        functools.partial(turn_kernel, parts),
        out_shape=[
            jax.ShapeDtypeStruct((width, rows), value.dtype),
            jax.ShapeDtypeStruct((parts, share, rows), value.dtype),
            jax.ShapeDtypeStruct((parts, share, rows), value.dtype),
        ],
        grid_spec=pltpu.PrefetchScalarGridSpec(
            num_scalar_prefetch=1,
            grid=(1,),
            in_specs=[pl.BlockSpec((rows, width), lambda i, s: (0, 0))],
            out_specs=[
                pl.BlockSpec((width, rows), lambda i, s: (0, 0)),
                pl.BlockSpec((parts, share, rows), lambda i, s: (0, 0, 0)),
                pl.BlockSpec((parts, share, rows), lambda i, s: (0, 0, 0)),
            ],
        ),
        compiler_params=pltpu.CompilerParams(vmem_limit_bytes=16 * 1024 * 1024),
        cost_estimate=pl.CostEstimate(
            flops=rows * width, bytes_accessed=8 * rows * width, transcendentals=0
        ),
        name="turn",
    )(sent_index, value)


def grad_kernel(parts, index_ref, *refs):
    mine, near = refs[:parts], refs[parts]
    own, nxt = refs[parts + 1][...], refs[parts + 2][...]
    outs = refs[parts + 3 :]
    for k in range(parts):
        total = jnp.dot(mine[k][...], own, preferred_element_type=jnp.float32)
        total = total + jnp.dot(near[k], nxt, preferred_element_type=jnp.float32)
        outs[k][...] = total.astype(outs[k].dtype)


def half_grad(index, turned, near, wide, next_half):
    parts, share, rows = near.shape
    half = next_half.shape[1]
    tile = tile_of(half, 512)
    per_half = half // tile

    def chosen(k):
        return pl.BlockSpec((share, rows), lambda i, s: (s[1 + k], 0))

    return pl.pallas_call(
        functools.partial(grad_kernel, parts),
        out_shape=[jax.ShapeDtypeStruct((share, half), jnp.bfloat16) for _ in range(parts)],
        grid_spec=pltpu.PrefetchScalarGridSpec(
            num_scalar_prefetch=1,
            grid=(per_half,),
            in_specs=[chosen(k) for k in range(parts)]
            + [
                pl.BlockSpec(near.shape, lambda i, s: (0, 0, 0)),
                pl.BlockSpec((rows, tile), lambda i, s: (0, s[0] * per_half + i)),
                pl.BlockSpec((rows, tile), lambda i, s: (0, i)),
            ],
            out_specs=[pl.BlockSpec((share, tile), lambda i, s: (0, i)) for _ in range(parts)],
        ),
        compiler_params=pltpu.CompilerParams(vmem_limit_bytes=32 * 1024 * 1024),
        cost_estimate=pl.CostEstimate(
            flops=4 * parts * share * rows * half,
            bytes_accessed=4 * rows * half + 2 * parts * share * half,
            transcendentals=0,
        ),
        name="half_grad",
    )(index, *([turned] * parts), near, wide, next_half)


def blank(shape):
    return pl.pallas_call(
        lambda out_ref: None,
        out_shape=jax.ShapeDtypeStruct(shape, jnp.bfloat16),
        out_specs=pl.BlockSpec(memory_space=pl.ANY),
    )()


def after(value, *needed):
    return lax.optimization_barrier((value, *needed))[0]


def step_kernel(parts, side_ref, accum_ref, *refs):
    pieces, out_ref, new_ref = refs[: 2 * parts], refs[-2], refs[-1]
    width = out_ref.shape[2]
    half = width // 2
    sums = []
    for h in range(2):
        total = pieces[h * parts][...].astype(jnp.float32)
        for k in range(1, parts):
            total = total + pieces[h * parts + k][...].astype(jnp.float32)
        sums.append(total)
    square = jnp.sum(sums[0] * sums[0], axis=1, keepdims=True) + jnp.sum(
        sums[1] * sums[1], axis=1, keepdims=True
    )
    renewed = accum_ref[...] + square * (1.0 / width)
    new_ref[...] = renewed
    root = jnp.sqrt(renewed)
    side = side_ref[0]
    near = pl.multiple_of(side * half, 128)
    far = pl.multiple_of((1 - side) * half, 128)
    out_ref[0, :, pl.ds(near, half)] = sums[0] / root
    out_ref[0, :, pl.ds(far, half)] = sums[1] / root


def weight_update(side, accum, near_parts, far_parts, layer_idx, depth, whole):
    parts = len(near_parts)
    share, half = near_parts[0].shape
    tile = 32
    piece = pl.BlockSpec((tile, half), lambda i, s: (i, 0))
    single = pl.BlockSpec((tile, 1), lambda i, s: (i, 0))
    carried = [] if whole is None else [whole]
    return pl.pallas_call(
        functools.partial(step_kernel, parts),
        out_shape=[
            jax.ShapeDtypeStruct((depth, share, 2 * half), jnp.float32),
            jax.ShapeDtypeStruct((share, 1), jnp.float32),
        ],
        grid_spec=pltpu.PrefetchScalarGridSpec(
            num_scalar_prefetch=1,
            grid=(share // tile,),
            in_specs=[single] + [piece] * (2 * parts) + [pl.BlockSpec(memory_space=pl.ANY)] * len(carried),
            out_specs=[
                pl.BlockSpec((1, tile, 2 * half), lambda i, s: (layer_idx, i, 0)),
                single,
            ],
        ),
        input_output_aliases={2 + 2 * parts: 0} if carried else {},
        compiler_params=pltpu.CompilerParams(vmem_limit_bytes=32 * 1024 * 1024),
        cost_estimate=pl.CostEstimate(
            flops=8 * share * half,
            bytes_accessed=share * half * (8 + 4 * parts),
            transcendentals=0,
        ),
        name="weight_update",
    )(side, accum, *near_parts, *far_parts, *carried)


def slot_kernel(embed, per_device, table_ref, summed_ref, late_ref, out_ref, joined):
    width = late_ref.shape[2]
    for m in range(late_ref.shape[0]):
        cols = slice(m * width, (m + 1) * width)
        joined[:, cols] = summed_ref[:, cols] + late_ref[m].astype(jnp.float32)
    devices, pairs, rows, lanes = out_ref.shape
    lane = lax.broadcasted_iota(jnp.int32, (rows, lanes), 1)

    def look(slot):
        first = table_ref[slot] * embed
        start = pl.multiple_of(first // lanes * lanes, 128)
        value = joined[:, pl.ds(start, lanes)]
        return value, first - start

    def one(device, carry):
        for p in range(pairs):
            slot = device * per_device + 2 * p
            low, low_at = look(slot)
            high, high_at = look(slot + min(1, per_device - 1 - 2 * p))
            low = jnp.where(low_at == 0, low, pltpu.roll(low, embed, 1))
            high = jnp.where(high_at == 0, pltpu.roll(high, embed, 1), high)
            out_ref[device, p] = jnp.where(lane < embed, low, high).astype(out_ref.dtype)
        return carry

    lax.fori_loop(0, devices, one, 0)


def to_slots(table_of, summed, late, embed, devices):
    rows = summed.shape[0]
    per_device = table_of.shape[0] // devices
    pairs = (per_device + 1) // 2
    return pl.pallas_call(
        functools.partial(slot_kernel, embed, per_device),
        out_shape=jax.ShapeDtypeStruct((devices, pairs, rows, 2 * embed), jnp.bfloat16),
        grid_spec=pltpu.PrefetchScalarGridSpec(
            num_scalar_prefetch=1,
            grid=(1,),
            in_specs=[
                pl.BlockSpec(summed.shape, lambda i, s: (0, 0)),
                pl.BlockSpec(late.shape, lambda i, s: (0, 0, 0)),
            ],
            out_specs=pl.BlockSpec((devices, pairs, rows, 2 * embed), lambda i, s: (0, 0, 0, 0)),
            scratch_shapes=[pltpu.VMEM(summed.shape, jnp.float32)],
        ),
        compiler_params=pltpu.CompilerParams(vmem_limit_bytes=32 * 1024 * 1024),
        cost_estimate=pl.CostEstimate(
            flops=4 * rows * summed.shape[1],
            bytes_accessed=10 * rows * summed.shape[1],
            transcendentals=0,
        ),
        name="to_slots",
    )(table_of, summed, late)


def body(
    features,
    cotangent,
    weights,
    biases,
    weight_accum,
    owner_slot,
    bag_ids,
    bag_length,
    tables,
    table_accum,
):
    depth, block_cols, full_width = weights.shape
    data_size = lax.axis_size("dp")
    model_size = lax.axis_size("mp")
    line = model_size // cores
    model_index = lax.axis_index("mp")
    data_index = lax.axis_index("dp")
    spot = model_index // cores
    core = model_index % cores
    first_core = core == 0
    rows = features.shape[0]
    half = full_width // 2
    members = data_size // 2
    f32, bf16 = jnp.float32, jnp.bfloat16

    def swap(value):
        return lax.ppermute(value, "mp", [(i, i ^ 1) for i in range(model_size)])

    def hop(value, right, left):
        pairs = [(z * cores, (z + 1) * cores) for z in right]
        pairs += [(z * cores + 1, (z - 1) * cores + 1) for z in left]
        return lax.ppermute(value, "mp", pairs)

    def chip_pair(value):
        other = swap(value)
        return jnp.where(
            first_core,
            jnp.concatenate([value, other], axis=1),
            jnp.concatenate([other, value], axis=1),
        )

    def gather_and_reduce(chip, partial_value, axis, fill):
        width = chip.shape[1]
        size = partial_value.shape[axis] // line
        part = size // cores

        def block(at):
            return lax.dynamic_slice_in_dim(
                partial_value, jnp.clip(at, 0, line - 1) * size, size, axis
            )

        wide = lax.dynamic_update_slice_in_dim(blank((rows, full_width)), chip, spot * width, 1)
        moving = hop(chip, range(0, line - 1), range(1, line))
        moving = after(moving, partial_value)
        inbound = None
        for k in range(1, line):
            passed = swap(moving)
            ahead = None
            if k + 1 < line:
                ahead = hop(moving, range(k, line - 1), range(1, line - k))
            far = line - k
            away = jnp.where(first_core, far, -far)
            crossed = swap(block(spot - away))
            total = block(spot + away).astype(f32) + crossed.astype(f32)
            if inbound is not None:
                total = total + inbound.astype(f32)
            total = total.astype(bf16)
            inbound = hop(total, range(k), range(line - k, line))
            for piece, up in ((moving, first_core), (passed, ~first_core)):
                place = jnp.where(up, spot - k, spot + k)
                here = (place >= 0) & (place < line)
                wide = lax.dynamic_update_slice_in_dim(
                    wide, jnp.where(here, piece, chip), jnp.where(here, place, spot) * width, 1
                )
            if ahead is not None:
                moving = after(ahead, total, *fill(k, total))

        def finish(*needed):
            last = after(inbound, *needed)
            local = block(spot)

            def portion(at):
                return lax.dynamic_slice_in_dim(local, at * part, part, axis).astype(
                    f32
                ) + lax.dynamic_slice_in_dim(last, at * part, part, axis).astype(f32)

            return portion(core) + swap(portion(1 - core).astype(bf16)).astype(f32)

        return wide, finish

    def crossing(low_core, high_core):
        pairs = []
        for d in range(data_size):
            for m in range(model_size):
                target = (high_core if m % cores else low_core)(d)
                pairs.append((d * model_size + m, target * model_size + m))
        return pairs

    def cross(value, low_core, high_core):
        return lax.ppermute(value, ("dp", "mp"), crossing(low_core, high_core))

    low_flip = lambda d: d ^ 1
    top_flip = lambda d: (d + members) % data_size
    low_turn = lambda k: lambda d: (d // 2 + k) % members * 2 + d % 2
    top_turn = lambda k: lambda d: d // members * members + (d % members + k) % members
    low_bit, low_rest = data_index % 2, data_index // 2
    top_bit, top_rest = data_index // members, data_index % members

    side = core.astype(jnp.int32)
    share = block_cols // data_size
    own_low = (first_core, ~first_core)

    def row_blocks(which, flip):
        turns = jnp.arange(members, dtype=jnp.int32)
        low = (low_rest + turns) % members * 2 + (low_bit ^ flip)
        top = (top_bit ^ flip) * members + (top_rest + turns) % members
        return jnp.where(own_low[which], low, top).astype(jnp.int32)

    sent_index = jnp.concatenate([row_blocks(0, 1), row_blocks(1, 1)])
    grad_index = [
        jnp.concatenate([(side if which == 0 else 1 - side)[None], row_blocks(which, 0)])
        for which in range(2)
    ]
    flips = ((low_flip, top_flip), (top_flip, low_flip))

    def layer_neighbour(wide, *needed):
        start = after(core * half, *needed)
        sent = lax.dynamic_slice_in_dim(wide, start, half, 1)
        near = cross(sent, *flips[0])
        return (near, swap(near)), sent

    def turned_sums(scaled, *needed):
        turned, own_sent, other_sent = turn(after(sent_index, *needed), scaled, members, share)
        return turned, cross(own_sent, *flips[0]), cross(other_sent, *flips[1])

    def half_sums(turned, wide, neighbours, *needed):
        result = []
        for which in range(2):
            pieces = half_grad(
                after(grad_index[which], *needed),
                turned[0],
                turned[1 + which],
                wide,
                neighbours[which],
            )
            arrived = [pieces[0]]
            for k in range(1, members):
                turns = (low_turn(k), top_turn(k))
                arrived.append(cross(pieces[k], *(turns if which == 0 else turns[::-1])))
            result.append(arrived)
        return result

    base_f32 = features.astype(f32)
    top_up = cotangent.astype(f32)

    def preact_of(wide, layer_idx):
        product = lax.dot_general(
            wide, weights[layer_idx], (((1,), (1,)), ((), ())), preferred_element_type=f32
        )
        return product + biases[layer_idx]

    def partial_of(scaled, layer_idx):
        return jnp.dot(scaled, weights[layer_idx], preferred_element_type=f32).astype(bf16)

    chip = chip_pair(features)
    top_scaled = (after(cotangent, chip).astype(f32) * base_f32).astype(bf16)
    top_turned = []

    def fill_top(k, total):
        if k == 1:
            top_turned.extend(turned_sums(top_scaled, total))
            return (top_turned[0],)
        return ()

    first_wide, low_up = gather_and_reduce(chip, partial_of(top_scaled, 1), 1, fill_top)
    first_pre = preact_of(first_wide, 0)
    current = (base_f32 * first_pre + base_f32).astype(bf16)
    low_up = top_up + low_up(current)
    first_near, first_sent = layer_neighbour(first_wide, current)
    chip = chip_pair(current)
    low_scaled = (after(low_up, chip, first_sent) * base_f32).astype(bf16)
    low_turned, low_sums = [], []

    def fill_low(k, total):
        if k == 1:
            low_turned.extend(turned_sums(low_scaled, total))
            return (low_turned[0],)
        if k == 2:
            low_sums.extend(half_sums(low_turned, first_wide, first_near, total))
            return (low_sums[0][0], low_sums[1][0])
        return ()

    second_wide, summed = gather_and_reduce(chip, partial_of(low_scaled, 0), 0, fill_low)
    second_pre = preact_of(second_wide, 1)
    late = (low_up + low_up * first_pre + top_up * second_pre).astype(bf16)
    summed = summed(late)
    second_near, second_sent = layer_neighbour(second_wide, late)
    late = lax.all_to_all(
        late.reshape(model_size, rows // model_size, block_cols),
        "mp",
        split_axis=0,
        concat_axis=0,
        tiled=True,
    )
    tables_all = owner_slot.shape[0]
    embed = full_width // tables_all
    table_of = (
        jnp.zeros((tables_all,), jnp.int32)
        .at[owner_slot]
        .set(jnp.arange(tables_all, dtype=jnp.int32))
    )
    slotted = to_slots(after(table_of, second_sent), summed, late, embed, data_size * model_size)
    arrived = lax.all_to_all(slotted, ("dp", "mp"), split_axis=0, concat_axis=0, tiled=True)
    top_sums = half_sums(top_turned, second_wide, second_near, slotted)
    whole, low_accum = weight_update(
        after(side[None], slotted), weight_accum[0][:, None], *low_sums, 0, depth, None
    )
    arrived = after(arrived, top_sums[0][0], top_sums[1][0], low_accum)

    _, batch, bag = bag_ids.shape
    vocab = tables.shape[1]
    in_bag = jnp.arange(bag, dtype=jnp.int32)[None, None, :] < bag_length[:, :, None]
    ids = jnp.where(in_bag, bag_ids, vocab).transpose(0, 2, 1).reshape(-1)
    new_tables, new_accum = embed_update(
        ids, arrived, jnp.swapaxes(tables, 1, 2), table_accum, bag, batch, learn_rate
    )
    whole, top_accum = weight_update(
        after(side[None], new_accum), weight_accum[1][:, None], *top_sums, 1, depth, whole
    )
    accums = jnp.stack([low_accum[:, 0], top_accum[:, 0]])
    return (whole, accums, jnp.swapaxes(new_tables, 1, 2), new_accum)


def solution(mesh):
    return jax.shard_map(
        body,
        mesh=mesh,
        in_specs=(
            P("dp", "mp"),
            P("dp", "mp"),
            P(None, "mp", None),
            P(None, "mp"),
            P(None, ("mp", "dp")),
            P(),
            P(("dp", "mp"), None, None),
            P(("dp", "mp"), None),
            P(("dp", "mp"), None, None),
            P(("dp", "mp"), None),
        ),
        out_specs=(
            P(None, ("mp", "dp"), None),
            P(None, ("mp", "dp")),
            P(("dp", "mp"), None, None),
            P(("dp", "mp"), None),
        ),
        check_vma=False,
    )
```

```python
import functools
import jax, jax.numpy as jnp
from jax import lax
from jax.experimental import pallas as pl
from jax.experimental.pallas import tpu as pltpu
from jax.sharding import PartitionSpec as P


learn_rate = 0.5
cores = 2


def embed_kernel(n_tab, bag, batch, embed, chunk, unroll, rate, ids_ref, g_ref, tab_ref, acc_in_ref, tab_out, acc_out, rows, *accs):
    step = pl.program_id(0)
    pairs = g_ref.shape[1]

    @pl.when(step == 0)
    def _():
        src, _, per, lanes = g_ref.shape
        for a in accs:
            a[...] = jnp.zeros_like(a)
        for p in range(pairs):
            rows[p] = g_ref[:, p].astype(jnp.float32).reshape(src * per, lanes)

        def one(i, carry):
            for u in range(unroll):
                b = i * unroll + u
                vals = [rows[p, pl.ds(b, 1), :] for p in range(pairs)]
                for j in range(bag):
                    for t in range(n_tab):
                        v = ids_ref[(t * bag + j) * batch + b]
                        accs[t + n_tab * (j % 2)][pl.ds(v, 1), :] += vals[t // 2]
            return carry

        lax.fori_loop(0, batch // unroll, one, 0)

    base = pl.multiple_of(step * chunk, chunk)
    for p in range(pairs):
        first = accs[2 * p][pl.ds(base, chunk), :] + accs[n_tab + 2 * p][pl.ds(base, chunk), :]
        if 2 * p + 1 < n_tab:
            second = accs[2 * p + 1][pl.ds(base, chunk), :] + accs[n_tab + 2 * p + 1][pl.ds(base, chunk), :]
            lane = lax.broadcasted_iota(jnp.int32, first.shape, 1)
            first = jnp.where(lane < embed, first, second)
        turned = first.T
        for o in range(min(2, n_tab - 2 * p)):
            t = 2 * p + o
            grad = turned[o * embed:(o + 1) * embed, :]
            renewed = acc_in_ref[t:t + 1, :] + jnp.sum(grad * grad, axis=0, keepdims=True) * (1.0 / embed)
            acc_out[t:t + 1, :] = renewed
            tab_out[t] = tab_ref[t] - grad * (rate / jnp.sqrt(renewed))


def embed_update(ids, grads, tables_t, accum, bag, batch, rate, chunk=2048, unroll=8):
    n_tab, embed, vocab = tables_t.shape
    chunk = min(chunk, vocab)
    kern = functools.partial(embed_kernel, n_tab, bag, batch, embed, chunk, unroll, rate)
    return pl.pallas_call(
        kern,
        out_shape=(jax.ShapeDtypeStruct(tables_t.shape, jnp.float32), jax.ShapeDtypeStruct(accum.shape, jnp.float32)),
        grid_spec=pltpu.PrefetchScalarGridSpec(
            num_scalar_prefetch=1,
            grid=(vocab // chunk,),
            in_specs=[
                pl.BlockSpec(grads.shape, lambda i, s: (0,) * 4, pipeline_mode=pl.Buffered(1)),
                pl.BlockSpec((n_tab, embed, chunk), lambda i, s: (0, 0, i)),
                pl.BlockSpec((n_tab, chunk), lambda i, s: (0, i)),
            ],
            out_specs=[
                pl.BlockSpec((n_tab, embed, chunk), lambda i, s: (0, 0, i)),
                pl.BlockSpec((n_tab, chunk), lambda i, s: (0, i)),
            ],
            scratch_shapes=[pltpu.VMEM((grads.shape[1], batch, grads.shape[3]), jnp.float32)]
            + [pltpu.VMEM((vocab + 8, grads.shape[3]), jnp.float32) for _ in range(2 * n_tab)],
        ),
        compiler_params=pltpu.CompilerParams(dimension_semantics=("arbitrary",), vmem_limit_bytes=56 * 1024 * 1024),
        cost_estimate=pl.CostEstimate(flops=100000000, bytes_accessed=150000000, transcendentals=0),
        name="embed_update",
    )(ids, grads, tables_t, accum)


def tile_of(size, limit):
    return max(t for t in range(128, limit + 1, 128) if size % t == 0)


def turn_kernel(parts, index_ref, value_ref, turned_ref, own_ref, other_ref):
    share = own_ref.shape[1]
    width = value_ref.shape[1]
    for first in range(0, width, 128):
        turned_ref[first : first + 128, :] = value_ref[:, first : first + 128].T
    for which, out in enumerate((own_ref, other_ref)):
        for k in range(parts):
            start = pl.multiple_of(index_ref[which * parts + k] * share, share)
            out[k] = turned_ref[pl.ds(start, share), :]


def turn(sent_index, value, parts, share):
    rows, width = value.shape
    return pl.pallas_call(
        functools.partial(turn_kernel, parts),
        out_shape=[
            jax.ShapeDtypeStruct((width, rows), value.dtype),
            jax.ShapeDtypeStruct((parts, share, rows), value.dtype),
            jax.ShapeDtypeStruct((parts, share, rows), value.dtype),
        ],
        grid_spec=pltpu.PrefetchScalarGridSpec(
            num_scalar_prefetch=1,
            grid=(1,),
            in_specs=[pl.BlockSpec((rows, width), lambda i, s: (0, 0))],
            out_specs=[
                pl.BlockSpec((width, rows), lambda i, s: (0, 0)),
                pl.BlockSpec((parts, share, rows), lambda i, s: (0, 0, 0)),
                pl.BlockSpec((parts, share, rows), lambda i, s: (0, 0, 0)),
            ],
        ),
        compiler_params=pltpu.CompilerParams(vmem_limit_bytes=16 * 1024 * 1024),
        cost_estimate=pl.CostEstimate(
            flops=rows * width, bytes_accessed=8 * rows * width, transcendentals=0
        ),
        name="turn",
    )(sent_index, value)


def grad_kernel(parts, index_ref, *refs):
    mine, near = refs[:parts], refs[parts]
    own, nxt = refs[parts + 1][...], refs[parts + 2][...]
    outs = refs[parts + 3 :]
    for k in range(parts):
        total = jnp.dot(mine[k][...], own, preferred_element_type=jnp.float32)
        total = total + jnp.dot(near[k], nxt, preferred_element_type=jnp.float32)
        outs[k][...] = total.astype(outs[k].dtype)


def half_grad(index, turned, near, wide, next_half):
    parts, share, rows = near.shape
    half = next_half.shape[1]
    tile = tile_of(half, 1024)
    per_half = half // tile

    def chosen(k):
        return pl.BlockSpec((share, rows), lambda i, s: (s[1 + k], 0))

    return pl.pallas_call(
        functools.partial(grad_kernel, parts),
        out_shape=[jax.ShapeDtypeStruct((share, half), jnp.bfloat16) for _ in range(parts)],
        grid_spec=pltpu.PrefetchScalarGridSpec(
            num_scalar_prefetch=1,
            grid=(per_half,),
            in_specs=[chosen(k) for k in range(parts)]
            + [
                pl.BlockSpec(near.shape, lambda i, s: (0, 0, 0)),
                pl.BlockSpec((rows, tile), lambda i, s: (0, s[0] * per_half + i)),
                pl.BlockSpec((rows, tile), lambda i, s: (0, i)),
            ],
            out_specs=[pl.BlockSpec((share, tile), lambda i, s: (0, i)) for _ in range(parts)],
        ),
        compiler_params=pltpu.CompilerParams(vmem_limit_bytes=32 * 1024 * 1024),
        cost_estimate=pl.CostEstimate(
            flops=4 * parts * share * rows * half,
            bytes_accessed=4 * rows * half + 2 * parts * share * half,
            transcendentals=0,
        ),
        name="half_grad",
    )(index, *([turned] * parts), near, wide, next_half)


def copy_kernel(index_ref, value_ref, out_ref):
    out_ref[...] = value_ref[...]


def column_half(side, value):
    rows, width = value.shape
    half = width // 2
    tile = rows // 4
    return pl.pallas_call(
        copy_kernel,
        out_shape=jax.ShapeDtypeStruct((rows, half), value.dtype),
        grid_spec=pltpu.PrefetchScalarGridSpec(
            num_scalar_prefetch=1,
            grid=(4,),
            in_specs=[pl.BlockSpec((tile, half), lambda i, s: (i, s[0]))],
            out_specs=pl.BlockSpec((tile, half), lambda i, s: (i, 0)),
        ),
        cost_estimate=pl.CostEstimate(
            flops=0, bytes_accessed=4 * rows * half, transcendentals=0
        ),
        name="column_half",
    )(side, value)


def blank(shape):
    return pl.pallas_call(
        lambda out_ref: None,
        out_shape=jax.ShapeDtypeStruct(shape, jnp.bfloat16),
        out_specs=pl.BlockSpec(memory_space=pl.ANY),
    )()


def after(value, *needed):
    return lax.optimization_barrier((value, *needed))[0]


def step_kernel(parts, side_ref, accum_ref, *refs):
    pieces, out_ref, new_ref = refs[: 2 * parts], refs[-2], refs[-1]
    width = out_ref.shape[2]
    half = width // 2
    sums = []
    for h in range(2):
        total = pieces[h * parts][...].astype(jnp.float32)
        for k in range(1, parts):
            total = total + pieces[h * parts + k][...].astype(jnp.float32)
        sums.append(total)
    square = jnp.sum(sums[0] * sums[0], axis=1, keepdims=True) + jnp.sum(
        sums[1] * sums[1], axis=1, keepdims=True
    )
    renewed = accum_ref[...] + square * (1.0 / width)
    new_ref[...] = renewed
    scale = 1.0 / jnp.sqrt(renewed)
    side = side_ref[0]
    near = pl.multiple_of(side * half, 128)
    far = pl.multiple_of((1 - side) * half, 128)
    out_ref[0, :, pl.ds(near, half)] = sums[0] * scale
    out_ref[0, :, pl.ds(far, half)] = sums[1] * scale


def weight_update(side, accum, near_parts, far_parts, layer_idx, depth, whole):
    parts = len(near_parts)
    share, half = near_parts[0].shape
    tile = 32
    piece = pl.BlockSpec((tile, half), lambda i, s: (i, 0))
    single = pl.BlockSpec((tile, 1), lambda i, s: (i, 0))
    carried = [] if whole is None else [whole]
    return pl.pallas_call(
        functools.partial(step_kernel, parts),
        out_shape=[
            jax.ShapeDtypeStruct((depth, share, 2 * half), jnp.float32),
            jax.ShapeDtypeStruct((share, 1), jnp.float32),
        ],
        grid_spec=pltpu.PrefetchScalarGridSpec(
            num_scalar_prefetch=1,
            grid=(share // tile,),
            in_specs=[single] + [piece] * (2 * parts) + [pl.BlockSpec(memory_space=pl.ANY)] * len(carried),
            out_specs=[
                pl.BlockSpec((1, tile, 2 * half), lambda i, s: (layer_idx, i, 0)),
                single,
            ],
        ),
        input_output_aliases={2 + 2 * parts: 0} if carried else {},
        compiler_params=pltpu.CompilerParams(vmem_limit_bytes=32 * 1024 * 1024),
        cost_estimate=pl.CostEstimate(
            flops=8 * share * half,
            bytes_accessed=share * half * (8 + 4 * parts),
            transcendentals=0,
        ),
        name="weight_update",
    )(side, accum, *near_parts, *far_parts, *carried)


def slot_kernel(embed, per_device, table_ref, summed_ref, late_ref, out_ref, joined):
    width = late_ref.shape[2]
    for m in range(late_ref.shape[0]):
        cols = slice(m * width, (m + 1) * width)
        joined[:, cols] = summed_ref[:, cols] + late_ref[m].astype(jnp.float32)
    devices, pairs, rows, lanes = out_ref.shape
    lane = lax.broadcasted_iota(jnp.int32, (rows, lanes), 1)

    def look(slot):
        first = table_ref[slot] * embed
        start = pl.multiple_of(first // lanes * lanes, 128)
        value = joined[:, pl.ds(start, lanes)]
        return value, first - start

    def one(device, carry):
        for p in range(pairs):
            slot = device * per_device + 2 * p
            low, low_at = look(slot)
            high, high_at = look(slot + min(1, per_device - 1 - 2 * p))
            low = jnp.where(low_at == 0, low, pltpu.roll(low, embed, 1))
            high = jnp.where(high_at == 0, pltpu.roll(high, embed, 1), high)
            out_ref[device, p] = jnp.where(lane < embed, low, high).astype(out_ref.dtype)
        return carry

    lax.fori_loop(0, devices, one, 0)


def to_slots(table_of, summed, late, embed, devices):
    rows = summed.shape[0]
    per_device = table_of.shape[0] // devices
    pairs = (per_device + 1) // 2
    return pl.pallas_call(
        functools.partial(slot_kernel, embed, per_device),
        out_shape=jax.ShapeDtypeStruct((devices, pairs, rows, 2 * embed), jnp.bfloat16),
        grid_spec=pltpu.PrefetchScalarGridSpec(
            num_scalar_prefetch=1,
            grid=(1,),
            in_specs=[
                pl.BlockSpec(summed.shape, lambda i, s: (0, 0)),
                pl.BlockSpec(late.shape, lambda i, s: (0, 0, 0)),
            ],
            out_specs=pl.BlockSpec((devices, pairs, rows, 2 * embed), lambda i, s: (0, 0, 0, 0)),
            scratch_shapes=[pltpu.VMEM(summed.shape, jnp.float32)],
        ),
        compiler_params=pltpu.CompilerParams(vmem_limit_bytes=32 * 1024 * 1024),
        cost_estimate=pl.CostEstimate(
            flops=4 * rows * summed.shape[1],
            bytes_accessed=10 * rows * summed.shape[1],
            transcendentals=0,
        ),
        name="to_slots",
    )(table_of, summed, late)


def body(
    features,
    cotangent,
    weights,
    biases,
    weight_accum,
    owner_slot,
    bag_ids,
    bag_length,
    tables,
    table_accum,
):
    depth, block_cols, full_width = weights.shape
    data_size = lax.axis_size("dp")
    model_size = lax.axis_size("mp")
    line = model_size // cores
    model_index = lax.axis_index("mp")
    data_index = lax.axis_index("dp")
    spot = model_index // cores
    core = model_index % cores
    first_core = core == 0
    rows = features.shape[0]
    members = data_size // 2
    f32, bf16 = jnp.float32, jnp.bfloat16

    def swap(value):
        return lax.ppermute(value, "mp", [(i, i ^ 1) for i in range(model_size)])

    def hop(value, right, left):
        pairs = [(z * cores, (z + 1) * cores) for z in right]
        pairs += [(z * cores + 1, (z - 1) * cores + 1) for z in left]
        return lax.ppermute(value, "mp", pairs)

    def chip_pair(value):
        other = swap(value)
        return jnp.where(
            first_core,
            jnp.concatenate([value, other], axis=1),
            jnp.concatenate([other, value], axis=1),
        )

    def gather_and_reduce(chip, partial_value, axis, fill, between, complete, gather_first):
        width = chip.shape[1]
        size = partial_value.shape[axis] // line
        part = size // cores

        def block(at):
            return lax.dynamic_slice_in_dim(
                partial_value, jnp.clip(at, 0, line - 1) * size, size, axis
            )

        wide = lax.dynamic_update_slice_in_dim(blank((rows, full_width)), chip, spot * width, 1)
        moving = hop(chip, range(0, line - 1), range(1, line))
        moving = after(moving, partial_value)
        inbound = None
        for k in range(1, line):
            passed = swap(moving)
            ahead = None
            if k + 1 < line:
                ahead = hop(moving, range(k, line - 1), range(1, line - k))
            for piece, up in ((moving, first_core), (passed, ~first_core)):
                place = jnp.where(up, spot - k, spot + k)
                here = (place >= 0) & (place < line)
                wide = lax.dynamic_update_slice_in_dim(
                    wide, jnp.where(here, piece, chip), jnp.where(here, place, spot) * width, 1
                )
            if k + 1 == line:
                inbound = after(inbound, *complete(wide))
            elif inbound is not None:
                inbound = after(inbound, *between(k, moving))
            far = line - k
            away = jnp.where(first_core, far, -far)
            theirs = spot - away
            if k == 1 and gather_first:
                theirs = after(theirs, moving)
            theirs = block(theirs)
            crossed = swap(theirs)
            total = block(spot + away).astype(f32) + crossed.astype(f32)
            if inbound is not None:
                total = total + inbound.astype(f32)
            total = total.astype(bf16)
            inbound = hop(total, range(k), range(line - k, line))
            if ahead is not None:
                moving = after(ahead, total, *fill(k, total, moving))

        def finish(*needed):
            last = after(inbound, *needed)
            local = block(spot)

            def portion(at):
                return lax.dynamic_slice_in_dim(local, at * part, part, axis).astype(
                    f32
                ) + lax.dynamic_slice_in_dim(last, at * part, part, axis).astype(f32)

            sent = portion(1 - core).astype(bf16)
            return portion(core) + swap(sent).astype(f32)

        return wide, finish

    def crossing(low_core, high_core):
        pairs = []
        for d in range(data_size):
            for m in range(model_size):
                target = (high_core if m % cores else low_core)(d)
                pairs.append((d * model_size + m, target * model_size + m))
        return pairs

    def cross(value, low_core, high_core):
        return lax.ppermute(value, ("dp", "mp"), crossing(low_core, high_core))

    low_flip = lambda d: d ^ 1
    top_flip = lambda d: (d + members) % data_size
    low_turn = lambda k: lambda d: (d // 2 + k) % members * 2 + d % 2
    top_turn = lambda k: lambda d: d // members * members + (d % members + k) % members
    low_bit, low_rest = data_index % 2, data_index // 2
    top_bit, top_rest = data_index // members, data_index % members

    side = core.astype(jnp.int32)
    share = block_cols // data_size
    own_low = (first_core, ~first_core)

    def row_blocks(which, flip):
        turns = jnp.arange(members, dtype=jnp.int32)
        low = (low_rest + turns) % members * 2 + (low_bit ^ flip)
        top = (top_bit ^ flip) * members + (top_rest + turns) % members
        return jnp.where(own_low[which], low, top).astype(jnp.int32)

    sent_index = jnp.concatenate([row_blocks(0, 1), row_blocks(1, 1)])
    grad_index = [
        jnp.concatenate([(side if which == 0 else 1 - side)[None], row_blocks(which, 0)])
        for which in range(2)
    ]
    flips = ((low_flip, top_flip), (top_flip, low_flip))

    def layer_neighbour(wide, *needed):
        sent = column_half(after(side[None], *needed), wide)
        near = cross(sent, *flips[0])
        return (near, swap(near)), sent

    def turned_sums(scaled, *needed):
        turned, own_sent, other_sent = turn(after(sent_index, *needed), scaled, members, share)
        return turned, cross(own_sent, *flips[0]), cross(other_sent, *flips[1])

    def half_sums(which, turned, wide, neighbours, *needed):
        pieces = half_grad(
            after(grad_index[which], *needed),
            turned[0],
            turned[1 + which],
            wide,
            neighbours[which],
        )
        arrived = [pieces[0]]
        for k in range(1, members):
            turns = (low_turn(k), top_turn(k))
            arrived.append(cross(pieces[k], *(turns if which == 0 else turns[::-1])))
        return arrived

    base_f32 = features.astype(f32)
    top_up = cotangent.astype(f32)
    none = lambda k, moving: ()

    def preact_of(wide, layer_idx):
        product = lax.dot_general(
            wide, weights[layer_idx], (((1,), (1,)), ((), ())), preferred_element_type=f32
        )
        return product + biases[layer_idx]

    def partial_of(scaled, layer_idx):
        return jnp.dot(scaled, weights[layer_idx], preferred_element_type=f32).astype(bf16)

    chip = chip_pair(features)
    top_scaled = (after(cotangent, chip).astype(f32) * base_f32).astype(bf16)
    top_turned = []

    def fill_top(k, total, moving):
        if k == 1:
            top_turned.extend(turned_sums(top_scaled, total))
            return (top_turned[0],)
        return ()

    nears = []

    def complete_top(wide):
        near, sent = layer_neighbour(wide)
        nears.append(near)
        return (sent,)

    def complete_low(wide):
        near, _ = layer_neighbour(wide)
        nears.append(near)
        return ()

    first_wide, low_up = gather_and_reduce(
        chip, partial_of(top_scaled, 1), 1, fill_top, none, complete_top, False
    )
    first_pre = preact_of(first_wide, 0)
    current = (base_f32 * first_pre + base_f32).astype(bf16)
    chip = chip_pair(current)
    low_up = top_up + low_up(chip)
    low_scaled = (after(low_up, chip) * base_f32).astype(bf16)
    low_turned, low_sums = [], []

    def fill_low(k, total, moving):
        if k == 1:
            low_turned.extend(turned_sums(low_scaled, moving))
            return (low_turned[0],)
        return ()

    def between_low(k, moving):
        if k == 2:
            low_sums.extend(
                half_sums(which, low_turned, first_wide, nears[0], moving)
                for which in range(2)
            )
            return (low_sums[0][0], low_sums[1][0])
        return ()

    second_wide, summed = gather_and_reduce(
        chip, partial_of(low_scaled, 0), 0, fill_low, between_low, complete_low, True
    )
    second_pre = preact_of(second_wide, 1)
    late = (low_up + low_up * first_pre + top_up * second_pre).astype(bf16)
    summed = summed(late)
    late_sent = late
    late = lax.all_to_all(
        late.reshape(model_size, rows // model_size, block_cols),
        "mp",
        split_axis=0,
        concat_axis=0,
        tiled=True,
    )
    tables_all = owner_slot.shape[0]
    embed = full_width // tables_all
    table_of = (
        jnp.zeros((tables_all,), jnp.int32)
        .at[owner_slot]
        .set(jnp.arange(tables_all, dtype=jnp.int32))
    )
    slotted = to_slots(table_of, summed, late, embed, data_size * model_size)
    arrived = lax.all_to_all(slotted, ("dp", "mp"), split_axis=0, concat_axis=0, tiled=True)
    top_sums = [half_sums(which, top_turned, second_wide, nears[1], slotted) for which in range(2)]
    whole, low_accum = weight_update(
        after(side[None], late_sent), weight_accum[0][:, None], *low_sums, 0, depth, None
    )
    arrived = after(arrived, top_sums[0][0], top_sums[1][0], low_accum)

    _, batch, bag = bag_ids.shape
    vocab = tables.shape[1]
    in_bag = jnp.arange(bag, dtype=jnp.int32)[None, None, :] < bag_length[:, :, None]
    ids = jnp.where(in_bag, bag_ids, vocab).transpose(0, 2, 1).reshape(-1)
    new_tables, new_accum = embed_update(
        ids, arrived, jnp.swapaxes(tables, 1, 2), table_accum, bag, batch, learn_rate
    )
    whole, top_accum = weight_update(
        after(side[None], new_accum), weight_accum[1][:, None], *top_sums, 1, depth, whole
    )
    accums = jnp.stack([low_accum[:, 0], top_accum[:, 0]])
    return (whole, accums, jnp.swapaxes(new_tables, 1, 2), new_accum)


def solution(mesh):
    return jax.shard_map(
        body,
        mesh=mesh,
        in_specs=(
            P("dp", "mp"),
            P("dp", "mp"),
            P(None, "mp", None),
            P(None, "mp"),
            P(None, ("mp", "dp")),
            P(),
            P(("dp", "mp"), None, None),
            P(("dp", "mp"), None),
            P(("dp", "mp"), None, None),
            P(("dp", "mp"), None),
        ),
        out_specs=(
            P(None, ("mp", "dp"), None),
            P(None, ("mp", "dp")),
            P(("dp", "mp"), None, None),
            P(("dp", "mp"), None),
        ),
        check_vma=False,
    )
```

```python
import functools
import jax, jax.numpy as jnp
from jax import lax
from jax.experimental import pallas as pl
from jax.experimental.pallas import tpu as pltpu
from jax.sharding import PartitionSpec as P


learn_rate = 0.5
cores = 2


def embed_kernel(n_tab, bag, batch, vocab, embed, chunk, unroll, rate, ids_ref, g_ref, tab_ref, acc_in_ref, tab_out, acc_out, rows, *accs):
    step = pl.program_id(0)
    pairs = g_ref.shape[1]

    @pl.when(step == 0)
    def _():
        src, _, per, lanes = g_ref.shape
        piece = min(256, vocab)

        def clear(i, carry):
            start = pl.multiple_of(i * piece, piece)
            for a in accs:
                a[pl.ds(start, piece), :] = jnp.zeros((piece, a.shape[1]), jnp.float32)
            return carry

        lax.fori_loop(0, vocab // piece, clear, 0)
        for p in range(pairs):
            rows[p] = g_ref[:, p].astype(jnp.float32).reshape(src * per, lanes)

        def one(i, carry):
            for u in range(unroll):
                b = i * unroll + u
                vals = [rows[p, pl.ds(b, 1), :] for p in range(pairs)]
                for j in range(bag):
                    for t in range(n_tab):
                        v = ids_ref[(t * bag + j) * batch + b]
                        accs[t + n_tab * (j % 2)][pl.ds(v, 1), :] += vals[t // 2]
            return carry

        lax.fori_loop(0, batch // unroll, one, 0)

    base = pl.multiple_of(step * chunk, chunk)
    for p in range(pairs):
        first = accs[2 * p][pl.ds(base, chunk), :] + accs[n_tab + 2 * p][pl.ds(base, chunk), :]
        if 2 * p + 1 < n_tab:
            second = accs[2 * p + 1][pl.ds(base, chunk), :] + accs[n_tab + 2 * p + 1][pl.ds(base, chunk), :]
            lane = lax.broadcasted_iota(jnp.int32, first.shape, 1)
            first = jnp.where(lane < embed, first, second)
        turned = first.T
        for o in range(min(2, n_tab - 2 * p)):
            t = 2 * p + o
            grad = turned[o * embed:(o + 1) * embed, :]
            renewed = acc_in_ref[t:t + 1, :] + jnp.sum(grad * grad, axis=0, keepdims=True) * (1.0 / embed)
            acc_out[t:t + 1, :] = renewed
            tab_out[t] = tab_ref[t] - grad * (rate / jnp.sqrt(renewed))


def embed_update(ids, grads, tables_t, accum, bag, batch, rate, chunk=2048, unroll=8):
    n_tab, embed, vocab = tables_t.shape
    chunk = min(chunk, vocab)
    kern = functools.partial(embed_kernel, n_tab, bag, batch, vocab, embed, chunk, unroll, rate)
    return pl.pallas_call(
        kern,
        out_shape=(jax.ShapeDtypeStruct(tables_t.shape, jnp.float32), jax.ShapeDtypeStruct(accum.shape, jnp.float32)),
        grid_spec=pltpu.PrefetchScalarGridSpec(
            num_scalar_prefetch=1,
            grid=(vocab // chunk,),
            in_specs=[
                pl.BlockSpec(grads.shape, lambda i, s: (0,) * 4, pipeline_mode=pl.Buffered(1)),
                pl.BlockSpec((n_tab, embed, chunk), lambda i, s: (0, 0, i)),
                pl.BlockSpec((n_tab, chunk), lambda i, s: (0, i)),
            ],
            out_specs=[
                pl.BlockSpec((n_tab, embed, chunk), lambda i, s: (0, 0, i)),
                pl.BlockSpec((n_tab, chunk), lambda i, s: (0, i)),
            ],
            scratch_shapes=[pltpu.VMEM((grads.shape[1], batch, grads.shape[3]), jnp.float32)]
            + [pltpu.VMEM((vocab + 8, grads.shape[3]), jnp.float32) for _ in range(2 * n_tab)],
        ),
        compiler_params=pltpu.CompilerParams(dimension_semantics=("arbitrary",), vmem_limit_bytes=56 * 1024 * 1024),
        cost_estimate=pl.CostEstimate(flops=100000000, bytes_accessed=150000000, transcendentals=0),
        name="embed_update",
    )(ids, grads, tables_t, accum)


def tile_of(size, limit):
    return max(t for t in range(128, limit + 1, 128) if size % t == 0)


def turn_kernel(parts, index_ref, value_ref, turned_ref, own_ref, other_ref):
    share = own_ref.shape[1]
    width = value_ref.shape[1]
    for first in range(0, width, 128):
        turned_ref[first : first + 128, :] = value_ref[:, first : first + 128].T
    for which, out in enumerate((own_ref, other_ref)):
        for k in range(parts):
            start = pl.multiple_of(index_ref[which * parts + k] * share, share)
            out[k] = turned_ref[pl.ds(start, share), :]


def turn(sent_index, value, parts, share):
    rows, width = value.shape
    return pl.pallas_call(
        functools.partial(turn_kernel, parts),
        out_shape=[
            jax.ShapeDtypeStruct((width, rows), value.dtype),
            jax.ShapeDtypeStruct((parts, share, rows), value.dtype),
            jax.ShapeDtypeStruct((parts, share, rows), value.dtype),
        ],
        grid_spec=pltpu.PrefetchScalarGridSpec(
            num_scalar_prefetch=1,
            grid=(1,),
            in_specs=[pl.BlockSpec((rows, width), lambda i, s: (0, 0))],
            out_specs=[
                pl.BlockSpec((width, rows), lambda i, s: (0, 0)),
                pl.BlockSpec((parts, share, rows), lambda i, s: (0, 0, 0)),
                pl.BlockSpec((parts, share, rows), lambda i, s: (0, 0, 0)),
            ],
        ),
        compiler_params=pltpu.CompilerParams(vmem_limit_bytes=16 * 1024 * 1024),
        cost_estimate=pl.CostEstimate(
            flops=rows * width, bytes_accessed=8 * rows * width, transcendentals=0
        ),
        name="turn",
    )(sent_index, value)


def grad_kernel(parts, index_ref, *refs):
    mine, near = refs[:parts], refs[parts]
    own, nxt = refs[parts + 1][...], refs[parts + 2][...]
    outs = refs[parts + 3 :]
    for k in range(parts):
        total = jnp.dot(mine[k][...], own, preferred_element_type=jnp.float32)
        total = total + jnp.dot(near[k], nxt, preferred_element_type=jnp.float32)
        outs[k][...] = total.astype(outs[k].dtype)


def half_grad(index, turned, near, wide, next_half):
    parts, share, rows = near.shape
    half = next_half.shape[1]
    tile = tile_of(half, 1024)
    per_half = half // tile

    def chosen(k):
        return pl.BlockSpec((share, rows), lambda i, s: (s[1 + k], 0))

    return pl.pallas_call(
        functools.partial(grad_kernel, parts),
        out_shape=[jax.ShapeDtypeStruct((share, half), jnp.bfloat16) for _ in range(parts)],
        grid_spec=pltpu.PrefetchScalarGridSpec(
            num_scalar_prefetch=1,
            grid=(per_half,),
            in_specs=[chosen(k) for k in range(parts)]
            + [
                pl.BlockSpec(near.shape, lambda i, s: (0, 0, 0)),
                pl.BlockSpec((rows, tile), lambda i, s: (0, s[0] * per_half + i)),
                pl.BlockSpec((rows, tile), lambda i, s: (0, i)),
            ],
            out_specs=[pl.BlockSpec((share, tile), lambda i, s: (0, i)) for _ in range(parts)],
        ),
        compiler_params=pltpu.CompilerParams(vmem_limit_bytes=32 * 1024 * 1024),
        cost_estimate=pl.CostEstimate(
            flops=4 * parts * share * rows * half,
            bytes_accessed=4 * rows * half + 2 * parts * share * half,
            transcendentals=0,
        ),
        name="half_grad",
    )(index, *([turned] * parts), near, wide, next_half)


def copy_kernel(index_ref, value_ref, out_ref):
    out_ref[...] = value_ref[...]


def column_half(side, value):
    rows, width = value.shape
    half = width // 2
    tile = rows // 4
    return pl.pallas_call(
        copy_kernel,
        out_shape=jax.ShapeDtypeStruct((rows, half), value.dtype),
        grid_spec=pltpu.PrefetchScalarGridSpec(
            num_scalar_prefetch=1,
            grid=(4,),
            in_specs=[pl.BlockSpec((tile, half), lambda i, s: (i, s[0]))],
            out_specs=pl.BlockSpec((tile, half), lambda i, s: (i, 0)),
        ),
        cost_estimate=pl.CostEstimate(
            flops=0, bytes_accessed=4 * rows * half, transcendentals=0
        ),
        name="column_half",
    )(side, value)


def columns_kernel(index_ref, value_ref, weight_ref, out_ref):
    out_ref[0] = jnp.dot(
        value_ref[...], weight_ref[0], preferred_element_type=jnp.float32
    ).astype(out_ref.dtype)


def column_blocks(index, value, weights, layer_idx, width):
    rows, depth = value.shape
    count = index.shape[0]
    tile = tile_of(width, 1024)
    steps = width // tile
    return pl.pallas_call(
        columns_kernel,
        out_shape=jax.ShapeDtypeStruct((count, rows, width), value.dtype),
        grid_spec=pltpu.PrefetchScalarGridSpec(
            num_scalar_prefetch=1,
            grid=(count, steps),
            in_specs=[
                pl.BlockSpec((rows, depth), lambda b, t, s: (0, 0)),
                pl.BlockSpec((1, depth, tile), lambda b, t, s: (layer_idx, 0, s[b] * steps + t)),
            ],
            out_specs=pl.BlockSpec((1, rows, tile), lambda b, t, s: (b, 0, t)),
        ),
        compiler_params=pltpu.CompilerParams(vmem_limit_bytes=24 * 1024 * 1024),
        cost_estimate=pl.CostEstimate(
            flops=2 * rows * depth * width * count,
            bytes_accessed=2 * width * count * (depth + rows),
            transcendentals=0,
        ),
        name="column_blocks",
    )(index, value, weights)


def rows_kernel(count, index_ref, *refs):
    weight_ref, out_ref = refs[count], refs[count + 1]
    value = jnp.concatenate([ref[...] for ref in refs[:count]], axis=0)
    product = jnp.dot(value, weight_ref[0], preferred_element_type=jnp.float32)
    out_ref[...] = product.astype(out_ref.dtype).reshape(out_ref.shape)


def row_blocks_product(index, value, weights, layer_idx):
    count = index.shape[0]
    rows, depth = value.shape
    size = rows // count
    width = weights.shape[2]
    tile = tile_of(width, 1024)

    def chosen(k):
        return pl.BlockSpec((size, depth), lambda i, s: (s[k], 0))

    return pl.pallas_call(
        functools.partial(rows_kernel, count),
        out_shape=jax.ShapeDtypeStruct((count, size, width), value.dtype),
        grid_spec=pltpu.PrefetchScalarGridSpec(
            num_scalar_prefetch=1,
            grid=(width // tile,),
            in_specs=[chosen(k) for k in range(count)]
            + [pl.BlockSpec((1, depth, tile), lambda i, s: (layer_idx, 0, i))],
            out_specs=pl.BlockSpec((count, size, tile), lambda i, s: (0, 0, i)),
        ),
        compiler_params=pltpu.CompilerParams(vmem_limit_bytes=24 * 1024 * 1024),
        cost_estimate=pl.CostEstimate(
            flops=2 * rows * depth * width,
            bytes_accessed=2 * width * (depth + rows),
            transcendentals=0,
        ),
        name="row_blocks_product",
    )(index, *([value] * count), weights)


def forward_kernel(wide_ref, weight_ref, bias_ref, out_ref):
    @pl.when(pl.program_id(0) == 0)
    def _():
        out_ref[...] = jnp.broadcast_to(bias_ref[...], out_ref.shape)

    out_ref[...] += lax.dot_general(
        wide_ref[...],
        weight_ref[0],
        (((1,), (1,)), ((), ())),
        preferred_element_type=jnp.float32,
    )


def forward_product(wide, weights, bias, layer_idx):
    rows, full = wide.shape
    width = weights.shape[1]
    tile = tile_of(full, 1024)
    return pl.pallas_call(
        forward_kernel,
        out_shape=jax.ShapeDtypeStruct((rows, width), jnp.float32),
        grid=(full // tile,),
        in_specs=[
            pl.BlockSpec((rows, tile), lambda i: (0, i)),
            pl.BlockSpec((1, width, tile), lambda i: (layer_idx, 0, i)),
            pl.BlockSpec((1, width), lambda i: (0, 0)),
        ],
        out_specs=pl.BlockSpec((rows, width), lambda i: (0, 0)),
        compiler_params=pltpu.CompilerParams(vmem_limit_bytes=24 * 1024 * 1024),
        cost_estimate=pl.CostEstimate(
            flops=2 * rows * full * width,
            bytes_accessed=2 * full * (rows + width),
            transcendentals=0,
        ),
        name="forward_product",
    )(wide, weights, bias[None])


def blank(shape):
    return pl.pallas_call(
        lambda out_ref: None,
        out_shape=jax.ShapeDtypeStruct(shape, jnp.bfloat16),
        out_specs=pl.BlockSpec(memory_space=pl.ANY),
    )()


def after(value, *needed):
    return lax.optimization_barrier((value, *needed))[0]


def step_kernel(parts, side_ref, accum_ref, *refs):
    pieces, out_ref, new_ref = refs[: 2 * parts], refs[-2], refs[-1]
    width = out_ref.shape[2]
    half = width // 2
    sums = []
    for h in range(2):
        total = pieces[h * parts][...].astype(jnp.float32)
        for k in range(1, parts):
            total = total + pieces[h * parts + k][...].astype(jnp.float32)
        sums.append(total)
    square = jnp.sum(sums[0] * sums[0], axis=1, keepdims=True) + jnp.sum(
        sums[1] * sums[1], axis=1, keepdims=True
    )
    renewed = accum_ref[...] + square * (1.0 / width)
    new_ref[...] = renewed
    scale = 1.0 / jnp.sqrt(renewed)
    side = side_ref[0]
    near = pl.multiple_of(side * half, 128)
    far = pl.multiple_of((1 - side) * half, 128)
    out_ref[0, :, pl.ds(near, half)] = sums[0] * scale
    out_ref[0, :, pl.ds(far, half)] = sums[1] * scale


def weight_update(side, accum, near_parts, far_parts, layer_idx, depth, whole):
    parts = len(near_parts)
    share, half = near_parts[0].shape
    tile = 32
    piece = pl.BlockSpec((tile, half), lambda i, s: (i, 0))
    single = pl.BlockSpec((tile, 1), lambda i, s: (i, 0))
    carried = [] if whole is None else [whole]
    return pl.pallas_call(
        functools.partial(step_kernel, parts),
        out_shape=[
            jax.ShapeDtypeStruct((depth, share, 2 * half), jnp.float32),
            jax.ShapeDtypeStruct((share, 1), jnp.float32),
        ],
        grid_spec=pltpu.PrefetchScalarGridSpec(
            num_scalar_prefetch=1,
            grid=(share // tile,),
            in_specs=[single] + [piece] * (2 * parts) + [pl.BlockSpec(memory_space=pl.ANY)] * len(carried),
            out_specs=[
                pl.BlockSpec((1, tile, 2 * half), lambda i, s: (layer_idx, i, 0)),
                single,
            ],
        ),
        input_output_aliases={2 + 2 * parts: 0} if carried else {},
        compiler_params=pltpu.CompilerParams(vmem_limit_bytes=32 * 1024 * 1024),
        cost_estimate=pl.CostEstimate(
            flops=8 * share * half,
            bytes_accessed=share * half * (8 + 4 * parts),
            transcendentals=0,
        ),
        name="weight_update",
    )(side, accum, *near_parts, *far_parts, *carried)


def slot_kernel(embed, per_device, table_ref, summed_ref, late_ref, out_ref, joined):
    width = late_ref.shape[2]
    for m in range(late_ref.shape[0]):
        cols = slice(m * width, (m + 1) * width)
        joined[:, cols] = summed_ref[:, cols] + late_ref[m].astype(jnp.float32)
    devices, pairs, rows, lanes = out_ref.shape
    lane = lax.broadcasted_iota(jnp.int32, (rows, lanes), 1)

    def look(slot):
        first = table_ref[slot] * embed
        start = pl.multiple_of(first // lanes * lanes, 128)
        value = joined[:, pl.ds(start, lanes)]
        return value, first - start

    def one(device, carry):
        for p in range(pairs):
            slot = device * per_device + 2 * p
            low, low_at = look(slot)
            high, high_at = look(slot + min(1, per_device - 1 - 2 * p))
            low = jnp.where(low_at == 0, low, pltpu.roll(low, embed, 1))
            high = jnp.where(high_at == 0, pltpu.roll(high, embed, 1), high)
            out_ref[device, p] = jnp.where(lane < embed, low, high).astype(out_ref.dtype)
        return carry

    lax.fori_loop(0, devices, one, 0)


def to_slots(table_of, summed, late, embed, devices):
    rows = summed.shape[0]
    per_device = table_of.shape[0] // devices
    pairs = (per_device + 1) // 2
    return pl.pallas_call(
        functools.partial(slot_kernel, embed, per_device),
        out_shape=jax.ShapeDtypeStruct((devices, pairs, rows, 2 * embed), jnp.bfloat16),
        grid_spec=pltpu.PrefetchScalarGridSpec(
            num_scalar_prefetch=1,
            grid=(1,),
            in_specs=[
                pl.BlockSpec(summed.shape, lambda i, s: (0, 0)),
                pl.BlockSpec(late.shape, lambda i, s: (0, 0, 0)),
            ],
            out_specs=pl.BlockSpec((devices, pairs, rows, 2 * embed), lambda i, s: (0, 0, 0, 0)),
            scratch_shapes=[pltpu.VMEM(summed.shape, jnp.float32)],
        ),
        compiler_params=pltpu.CompilerParams(vmem_limit_bytes=32 * 1024 * 1024),
        cost_estimate=pl.CostEstimate(
            flops=4 * rows * summed.shape[1],
            bytes_accessed=10 * rows * summed.shape[1],
            transcendentals=0,
        ),
        name="to_slots",
    )(table_of, summed, late)


def body(
    features,
    cotangent,
    weights,
    biases,
    weight_accum,
    owner_slot,
    bag_ids,
    bag_length,
    tables,
    table_accum,
):
    depth, block_cols, full_width = weights.shape
    data_size = lax.axis_size("dp")
    model_size = lax.axis_size("mp")
    line = model_size // cores
    model_index = lax.axis_index("mp")
    data_index = lax.axis_index("dp")
    spot = model_index // cores
    core = model_index % cores
    first_core = core == 0
    rows = features.shape[0]
    members = data_size // 2
    f32, bf16 = jnp.float32, jnp.bfloat16

    def swap(value):
        return lax.ppermute(value, "mp", [(i, i ^ 1) for i in range(model_size)])

    def hop(value, right, left):
        pairs = [(z * cores, (z + 1) * cores) for z in right]
        pairs += [(z * cores + 1, (z - 1) * cores + 1) for z in left]
        return lax.ppermute(value, "mp", pairs)

    def chip_pair(value):
        other = swap(value)
        return jnp.where(
            first_core,
            jnp.concatenate([value, other], axis=1),
            jnp.concatenate([other, value], axis=1),
        )

    def selected(held, k):
        up, down = held[line - k], held[k]
        if 2 * k == line:
            return up, down
        return jnp.where(first_core, up, down), jnp.where(first_core, down, up)

    def chips(offsets):
        return jnp.stack([(spot + j) % line for j in offsets]).astype(jnp.int32)

    def by_columns(scaled, layer_idx):
        width = cores * block_cols
        held = {}

        def products(offsets, *needed):
            product = column_blocks(
                after(chips(offsets), *needed), scaled, weights, layer_idx, width
            )
            for at, j in enumerate(offsets):
                held[j] = product[at]
            return product

        first = products((1, line - 1))
        rest = lambda sent: (products((*range(2, line - 1), 0), sent),)
        return first, lambda k: selected(held, k), lambda: held[0], rest

    def by_rows(scaled, layer_idx):
        product = row_blocks_product(chips(range(line)), scaled, weights, layer_idx)
        held = [product[j] for j in range(line)]
        return product, lambda k: selected(held, k), lambda: held[0], lambda sent: ()

    def gather_and_reduce(chip, partial, axis, fill, between, complete, reduce_first):
        width = chip.shape[1]
        first, pair, own, rest = partial
        wide = lax.dynamic_update_slice_in_dim(blank((rows, full_width)), chip, spot * width, 1)
        moving = hop(chip, range(0, line - 1), range(1, line))
        moving = after(moving, first)
        inbound, ready = None, None
        if reduce_first:
            mine, theirs = pair(1)
            crossed = after(swap(theirs), *rest(theirs))
            ready = (mine.astype(f32) + crossed.astype(f32)).astype(bf16)
            moving = after(moving, ready)
        for k in range(1, line):
            passed = swap(moving)
            ahead = None
            if k + 1 < line:
                ahead = hop(moving, range(k, line - 1), range(1, line - k))
            for piece, up in ((moving, first_core), (passed, ~first_core)):
                place = jnp.where(up, spot - k, spot + k)
                here = (place >= 0) & (place < line)
                wide = lax.dynamic_update_slice_in_dim(
                    wide, jnp.where(here, piece, chip), jnp.where(here, place, spot) * width, 1
                )
            if k + 1 == line:
                inbound = after(inbound, *complete(wide))
            elif inbound is not None:
                inbound = after(inbound, *between(k, moving))
            if ready is not None:
                total, ready = ready, None
            else:
                mine, theirs = pair(k)
                crossed = swap(theirs)
                total = mine.astype(f32) + crossed.astype(f32)
                if inbound is not None:
                    total = total + inbound.astype(f32)
                total = total.astype(bf16)
            inbound = hop(total, range(k), range(line - k, line))
            if ahead is not None:
                moving = after(ahead, total, *fill(k, total, moving))

        def finish(*needed):
            last = after(inbound, *needed)
            local = own()
            part = local.shape[axis] // cores

            def portion(at):
                return lax.dynamic_slice_in_dim(local, at * part, part, axis).astype(
                    f32
                ) + lax.dynamic_slice_in_dim(last, at * part, part, axis).astype(f32)

            sent = portion(1 - core).astype(bf16)
            return portion(core) + swap(sent).astype(f32)

        return wide, finish

    def crossing(low_core, high_core):
        pairs = []
        for d in range(data_size):
            for m in range(model_size):
                target = (high_core if m % cores else low_core)(d)
                pairs.append((d * model_size + m, target * model_size + m))
        return pairs

    def cross(value, low_core, high_core):
        return lax.ppermute(value, ("dp", "mp"), crossing(low_core, high_core))

    low_flip = lambda d: d ^ 1
    top_flip = lambda d: (d + members) % data_size
    low_turn = lambda k: lambda d: (d // 2 + k) % members * 2 + d % 2
    top_turn = lambda k: lambda d: d // members * members + (d % members + k) % members
    low_bit, low_rest = data_index % 2, data_index // 2
    top_bit, top_rest = data_index // members, data_index % members

    side = core.astype(jnp.int32)
    share = block_cols // data_size
    own_low = (first_core, ~first_core)

    def row_blocks(which, flip):
        turns = jnp.arange(members, dtype=jnp.int32)
        low = (low_rest + turns) % members * 2 + (low_bit ^ flip)
        top = (top_bit ^ flip) * members + (top_rest + turns) % members
        return jnp.where(own_low[which], low, top).astype(jnp.int32)

    sent_index = jnp.concatenate([row_blocks(0, 1), row_blocks(1, 1)])
    grad_index = [
        jnp.concatenate([(side if which == 0 else 1 - side)[None], row_blocks(which, 0)])
        for which in range(2)
    ]
    flips = ((low_flip, top_flip), (top_flip, low_flip))

    def layer_neighbour(wide, *needed):
        sent = column_half(after(side[None], *needed), wide)
        near = cross(sent, *flips[0])
        return (near, swap(near)), sent

    def turned_sums(scaled, *needed):
        turned, own_sent, other_sent = turn(after(sent_index, *needed), scaled, members, share)
        return turned, cross(own_sent, *flips[0]), cross(other_sent, *flips[1])

    def half_sums(which, turned, wide, neighbours, *needed):
        pieces = half_grad(
            after(grad_index[which], *needed),
            turned[0],
            turned[1 + which],
            wide,
            neighbours[which],
        )
        arrived = [pieces[0]]
        for k in range(1, members):
            turns = (low_turn(k), top_turn(k))
            arrived.append(cross(pieces[k], *(turns if which == 0 else turns[::-1])))
        return arrived

    base_f32 = features.astype(f32)
    top_up = cotangent.astype(f32)
    none = lambda k, moving: ()

    def preact_of(wide, layer_idx):
        return forward_product(wide, weights, biases[layer_idx], layer_idx)

    chip = chip_pair(features)
    top_scaled = (after(cotangent, chip).astype(f32) * base_f32).astype(bf16)
    top_turned = []

    def fill_top(k, total, moving):
        if k == 1:
            top_turned.extend(turned_sums(top_scaled, total))
            return (top_turned[0],)
        return ()

    nears = []

    def complete_top(wide):
        near, sent = layer_neighbour(wide)
        nears.append(near)
        return (sent,)

    def complete_low(wide):
        near, sent = layer_neighbour(wide)
        nears.append(near)
        return (sent,)

    first_wide, low_up = gather_and_reduce(
        chip, by_columns(top_scaled, 1), 1, fill_top, none, complete_top, True
    )
    first_pre = preact_of(first_wide, 0)
    current = (base_f32 * first_pre + base_f32).astype(bf16)
    chip = chip_pair(current)
    low_up = top_up + low_up(chip)
    low_scaled = (after(low_up, chip) * base_f32).astype(bf16)
    low_turned, low_sums = [], []

    def fill_low(k, total, moving):
        if k == 1:
            low_turned.extend(turned_sums(low_scaled, moving))
            return (low_turned[0],)
        if k == 2:
            low_half(1, total)
        return ()

    def low_half(which, *needed):
        low_sums.append(half_sums(which, low_turned, first_wide, nears[0], *needed))
        return (low_sums[which][0],)

    def between_low(k, moving):
        return low_half(0, moving) if k == 2 else ()

    second_wide, summed = gather_and_reduce(
        chip, by_rows(low_scaled, 0), 0, fill_low, between_low, complete_low, False
    )
    second_pre = preact_of(second_wide, 1)
    late = (low_up + low_up * first_pre + top_up * second_pre).astype(bf16)
    summed = summed(late)
    late_sent = late
    late = lax.all_to_all(
        late.reshape(model_size, rows // model_size, block_cols),
        "mp",
        split_axis=0,
        concat_axis=0,
        tiled=True,
    )
    tables_all = owner_slot.shape[0]
    embed = full_width // tables_all
    table_of = (
        jnp.zeros((tables_all,), jnp.int32)
        .at[owner_slot]
        .set(jnp.arange(tables_all, dtype=jnp.int32))
    )
    slotted = to_slots(table_of, summed, late, embed, data_size * model_size)
    arrived = lax.all_to_all(slotted, ("dp", "mp"), split_axis=0, concat_axis=0, tiled=True)
    top_sums = [half_sums(which, top_turned, second_wide, nears[1], slotted) for which in range(2)]
    whole, low_accum = weight_update(
        after(side[None], late_sent), weight_accum[0][:, None], *low_sums, 0, depth, None
    )
    arrived = after(arrived, top_sums[0][0], top_sums[1][0], low_accum)

    _, batch, bag = bag_ids.shape
    vocab = tables.shape[1]
    in_bag = jnp.arange(bag, dtype=jnp.int32)[None, None, :] < bag_length[:, :, None]
    ids = jnp.where(in_bag, bag_ids, vocab).transpose(0, 2, 1).reshape(-1)
    new_tables, new_accum = embed_update(
        ids, arrived, jnp.swapaxes(tables, 1, 2), table_accum, bag, batch, learn_rate
    )
    whole, top_accum = weight_update(
        after(side[None], new_accum), weight_accum[1][:, None], *top_sums, 1, depth, whole
    )
    accums = jnp.stack([low_accum[:, 0], top_accum[:, 0]])
    return (whole, accums, jnp.swapaxes(new_tables, 1, 2), new_accum)


def solution(mesh):
    return jax.shard_map(
        body,
        mesh=mesh,
        in_specs=(
            P("dp", "mp"),
            P("dp", "mp"),
            P(None, "mp", None),
            P(None, "mp"),
            P(None, ("mp", "dp")),
            P(),
            P(("dp", "mp"), None, None),
            P(("dp", "mp"), None),
            P(("dp", "mp"), None, None),
            P(("dp", "mp"), None),
        ),
        out_specs=(
            P(None, ("mp", "dp"), None),
            P(None, ("mp", "dp")),
            P(("dp", "mp"), None, None),
            P(("dp", "mp"), None),
        ),
        check_vma=False,
    )
```

```python
import functools
import jax, jax.numpy as jnp
from jax import lax
from jax.experimental import pallas as pl
from jax.experimental.pallas import tpu as pltpu
from jax.sharding import PartitionSpec as P


learn_rate = 0.5
cores = 2


def embed_kernel(n_tab, bag, batch, vocab, embed, chunk, unroll, rate, ids_ref, g_ref, tab_ref, acc_in_ref, tab_out, acc_out, rows, *accs):
    step = pl.program_id(0)
    pairs = g_ref.shape[1]

    @pl.when(step == 0)
    def _():
        src, _, per, lanes = g_ref.shape
        piece = min(256, vocab)

        def clear(i, carry):
            start = pl.multiple_of(i * piece, piece)
            for a in accs:
                a[pl.ds(start, piece), :] = jnp.zeros((piece, a.shape[1]), jnp.float32)
            return carry

        lax.fori_loop(0, vocab // piece, clear, 0)
        for p in range(pairs):
            rows[p] = g_ref[:, p].astype(jnp.float32).reshape(src * per, lanes)

        def one(i, carry):
            for u in range(unroll):
                b = i * unroll + u
                vals = [rows[p, pl.ds(b, 1), :] for p in range(pairs)]
                for j in range(bag):
                    for t in range(n_tab):
                        v = ids_ref[(t * bag + j) * batch + b]
                        accs[t + n_tab * (j % 2)][pl.ds(v, 1), :] += vals[t // 2]
            return carry

        lax.fori_loop(0, batch // unroll, one, 0)

    base = pl.multiple_of(step * chunk, chunk)
    for p in range(pairs):
        first = accs[2 * p][pl.ds(base, chunk), :] + accs[n_tab + 2 * p][pl.ds(base, chunk), :]
        if 2 * p + 1 < n_tab:
            second = accs[2 * p + 1][pl.ds(base, chunk), :] + accs[n_tab + 2 * p + 1][pl.ds(base, chunk), :]
            lane = lax.broadcasted_iota(jnp.int32, first.shape, 1)
            first = jnp.where(lane < embed, first, second)
        turned = first.T
        for o in range(min(2, n_tab - 2 * p)):
            t = 2 * p + o
            grad = turned[o * embed:(o + 1) * embed, :]
            renewed = acc_in_ref[t:t + 1, :] + jnp.sum(grad * grad, axis=0, keepdims=True) * (1.0 / embed)
            acc_out[t:t + 1, :] = renewed
            tab_out[t] = tab_ref[t] - grad * (rate / jnp.sqrt(renewed))


def embed_update(ids, grads, tables_t, accum, bag, batch, rate, chunk=2048, unroll=8):
    n_tab, embed, vocab = tables_t.shape
    chunk = min(chunk, vocab)
    kern = functools.partial(embed_kernel, n_tab, bag, batch, vocab, embed, chunk, unroll, rate)
    return pl.pallas_call(
        kern,
        out_shape=(jax.ShapeDtypeStruct(tables_t.shape, jnp.float32), jax.ShapeDtypeStruct(accum.shape, jnp.float32)),
        grid_spec=pltpu.PrefetchScalarGridSpec(
            num_scalar_prefetch=1,
            grid=(vocab // chunk,),
            in_specs=[
                pl.BlockSpec(grads.shape, lambda i, s: (0,) * 4, pipeline_mode=pl.Buffered(1)),
                pl.BlockSpec((n_tab, embed, chunk), lambda i, s: (0, 0, i)),
                pl.BlockSpec((n_tab, chunk), lambda i, s: (0, i)),
            ],
            out_specs=[
                pl.BlockSpec((n_tab, embed, chunk), lambda i, s: (0, 0, i)),
                pl.BlockSpec((n_tab, chunk), lambda i, s: (0, i)),
            ],
            scratch_shapes=[pltpu.VMEM((grads.shape[1], batch, grads.shape[3]), jnp.float32)]
            + [pltpu.VMEM((vocab + 8, grads.shape[3]), jnp.float32) for _ in range(2 * n_tab)],
        ),
        compiler_params=pltpu.CompilerParams(dimension_semantics=("arbitrary",), vmem_limit_bytes=56 * 1024 * 1024),
        cost_estimate=pl.CostEstimate(flops=100000000, bytes_accessed=150000000, transcendentals=0),
        name="embed_update",
    )(ids, grads, tables_t, accum)


def tile_of(size, limit):
    return max(t for t in range(128, limit + 1, 128) if size % t == 0)


def turn_kernel(parts, index_ref, value_ref, turned_ref, own_ref, other_ref):
    share = own_ref.shape[1]
    width = value_ref.shape[1]
    for first in range(0, width, 128):
        turned_ref[first : first + 128, :] = value_ref[:, first : first + 128].T
    for which, out in enumerate((own_ref, other_ref)):
        for k in range(parts):
            start = pl.multiple_of(index_ref[which * parts + k] * share, share)
            out[k] = turned_ref[pl.ds(start, share), :]


def turn(sent_index, value, parts, share):
    rows, width = value.shape
    return pl.pallas_call(
        functools.partial(turn_kernel, parts),
        out_shape=[
            jax.ShapeDtypeStruct((width, rows), value.dtype),
            jax.ShapeDtypeStruct((parts, share, rows), value.dtype),
            jax.ShapeDtypeStruct((parts, share, rows), value.dtype),
        ],
        grid_spec=pltpu.PrefetchScalarGridSpec(
            num_scalar_prefetch=1,
            grid=(1,),
            in_specs=[pl.BlockSpec((rows, width), lambda i, s: (0, 0))],
            out_specs=[
                pl.BlockSpec((width, rows), lambda i, s: (0, 0)),
                pl.BlockSpec((parts, share, rows), lambda i, s: (0, 0, 0)),
                pl.BlockSpec((parts, share, rows), lambda i, s: (0, 0, 0)),
            ],
        ),
        compiler_params=pltpu.CompilerParams(vmem_limit_bytes=16 * 1024 * 1024),
        cost_estimate=pl.CostEstimate(
            flops=rows * width, bytes_accessed=8 * rows * width, transcendentals=0
        ),
        name="turn",
    )(sent_index, value)


def grad_kernel(parts, index_ref, *refs):
    mine, near = refs[:parts], refs[parts]
    own, nxt = refs[parts + 1][...], refs[parts + 2][...]
    outs = refs[parts + 3 :]
    for k in range(parts):
        total = jnp.dot(mine[k][...], own, preferred_element_type=jnp.float32)
        total = total + jnp.dot(near[k], nxt, preferred_element_type=jnp.float32)
        outs[k][...] = total.astype(outs[k].dtype)


def half_grad(index, turned, near, wide, next_half):
    parts, share, rows = near.shape
    half = next_half.shape[1]
    tile = tile_of(half, 1024)
    per_half = half // tile

    def chosen(k):
        return pl.BlockSpec((share, rows), lambda i, s: (s[1 + k], 0))

    return pl.pallas_call(
        functools.partial(grad_kernel, parts),
        out_shape=[jax.ShapeDtypeStruct((share, half), jnp.bfloat16) for _ in range(parts)],
        grid_spec=pltpu.PrefetchScalarGridSpec(
            num_scalar_prefetch=1,
            grid=(per_half,),
            in_specs=[chosen(k) for k in range(parts)]
            + [
                pl.BlockSpec(near.shape, lambda i, s: (0, 0, 0)),
                pl.BlockSpec((rows, tile), lambda i, s: (0, s[0] * per_half + i)),
                pl.BlockSpec((rows, tile), lambda i, s: (0, i)),
            ],
            out_specs=[pl.BlockSpec((share, tile), lambda i, s: (0, i)) for _ in range(parts)],
        ),
        compiler_params=pltpu.CompilerParams(vmem_limit_bytes=32 * 1024 * 1024),
        cost_estimate=pl.CostEstimate(
            flops=4 * parts * share * rows * half,
            bytes_accessed=4 * rows * half + 2 * parts * share * half,
            transcendentals=0,
        ),
        name="half_grad",
    )(index, *([turned] * parts), near, wide, next_half)


def copy_kernel(index_ref, value_ref, out_ref):
    out_ref[...] = value_ref[...]


def column_half(side, value):
    rows, width = value.shape
    half = width // 2
    tile = rows // 4
    return pl.pallas_call(
        copy_kernel,
        out_shape=jax.ShapeDtypeStruct((rows, half), value.dtype),
        grid_spec=pltpu.PrefetchScalarGridSpec(
            num_scalar_prefetch=1,
            grid=(4,),
            in_specs=[pl.BlockSpec((tile, half), lambda i, s: (i, s[0]))],
            out_specs=pl.BlockSpec((tile, half), lambda i, s: (i, 0)),
        ),
        cost_estimate=pl.CostEstimate(
            flops=0, bytes_accessed=4 * rows * half, transcendentals=0
        ),
        name="column_half",
    )(side, value)


def columns_kernel(index_ref, value_ref, weight_ref, out_ref):
    out_ref[0] = jnp.dot(
        value_ref[...], weight_ref[0], preferred_element_type=jnp.float32
    ).astype(out_ref.dtype)


def column_blocks(index, value, weights, layer_idx, width):
    rows, depth = value.shape
    count = index.shape[0]
    tile = tile_of(width, 1024)
    steps = width // tile
    return pl.pallas_call(
        columns_kernel,
        out_shape=jax.ShapeDtypeStruct((count, rows, width), value.dtype),
        grid_spec=pltpu.PrefetchScalarGridSpec(
            num_scalar_prefetch=1,
            grid=(count, steps),
            in_specs=[
                pl.BlockSpec((rows, depth), lambda b, t, s: (0, 0)),
                pl.BlockSpec((1, depth, tile), lambda b, t, s: (layer_idx, 0, s[b] * steps + t)),
            ],
            out_specs=pl.BlockSpec((1, rows, tile), lambda b, t, s: (b, 0, t)),
        ),
        compiler_params=pltpu.CompilerParams(vmem_limit_bytes=24 * 1024 * 1024),
        cost_estimate=pl.CostEstimate(
            flops=2 * rows * depth * width * count,
            bytes_accessed=2 * width * count * (depth + rows),
            transcendentals=0,
        ),
        name="column_blocks",
    )(index, value, weights)


def rows_kernel(count, index_ref, *refs):
    weight_ref, out_ref = refs[count], refs[count + 1]
    value = jnp.concatenate([ref[...] for ref in refs[:count]], axis=0)
    product = jnp.dot(value, weight_ref[0], preferred_element_type=jnp.float32)
    out_ref[...] = product.astype(out_ref.dtype).reshape(out_ref.shape)


def row_blocks_product(index, value, weights, layer_idx):
    count = index.shape[0]
    rows, depth = value.shape
    size = rows // count
    width = weights.shape[2]
    tile = tile_of(width, 1024)

    def chosen(k):
        return pl.BlockSpec((size, depth), lambda i, s: (s[k], 0))

    return pl.pallas_call(
        functools.partial(rows_kernel, count),
        out_shape=jax.ShapeDtypeStruct((count, size, width), value.dtype),
        grid_spec=pltpu.PrefetchScalarGridSpec(
            num_scalar_prefetch=1,
            grid=(width // tile,),
            in_specs=[chosen(k) for k in range(count)]
            + [pl.BlockSpec((1, depth, tile), lambda i, s: (layer_idx, 0, i))],
            out_specs=pl.BlockSpec((count, size, tile), lambda i, s: (0, 0, i)),
        ),
        compiler_params=pltpu.CompilerParams(vmem_limit_bytes=24 * 1024 * 1024),
        cost_estimate=pl.CostEstimate(
            flops=2 * rows * depth * width,
            bytes_accessed=2 * width * (depth + rows),
            transcendentals=0,
        ),
        name="row_blocks_product",
    )(index, *([value] * count), weights)


def forward_kernel(wide_ref, weight_ref, bias_ref, out_ref):
    @pl.when(pl.program_id(0) == 0)
    def _():
        out_ref[...] = jnp.broadcast_to(bias_ref[...], out_ref.shape)

    out_ref[...] += lax.dot_general(
        wide_ref[...],
        weight_ref[0],
        (((1,), (1,)), ((), ())),
        preferred_element_type=jnp.float32,
    )


def forward_product(wide, weights, bias, layer_idx):
    rows, full = wide.shape
    width = weights.shape[1]
    tile = tile_of(full, 1024)
    return pl.pallas_call(
        forward_kernel,
        out_shape=jax.ShapeDtypeStruct((rows, width), jnp.float32),
        grid=(full // tile,),
        in_specs=[
            pl.BlockSpec((rows, tile), lambda i: (0, i)),
            pl.BlockSpec((1, width, tile), lambda i: (layer_idx, 0, i)),
            pl.BlockSpec((1, width), lambda i: (0, 0)),
        ],
        out_specs=pl.BlockSpec((rows, width), lambda i: (0, 0)),
        compiler_params=pltpu.CompilerParams(vmem_limit_bytes=24 * 1024 * 1024),
        cost_estimate=pl.CostEstimate(
            flops=2 * rows * full * width,
            bytes_accessed=2 * full * (rows + width),
            transcendentals=0,
        ),
        name="forward_product",
    )(wide, weights, bias[None])


def blank(shape):
    return pl.pallas_call(
        lambda out_ref: None,
        out_shape=jax.ShapeDtypeStruct(shape, jnp.bfloat16),
        out_specs=pl.BlockSpec(memory_space=pl.ANY),
    )()


def after(value, *needed):
    return lax.optimization_barrier((value, *needed))[0]


def step_kernel(parts, side_ref, accum_ref, *refs):
    pieces, out_ref, new_ref = refs[: 2 * parts], refs[-2], refs[-1]
    width = out_ref.shape[2]
    half = width // 2
    sums = []
    for h in range(2):
        total = pieces[h * parts][...].astype(jnp.float32)
        for k in range(1, parts):
            total = total + pieces[h * parts + k][...].astype(jnp.float32)
        sums.append(total)
    square = jnp.sum(sums[0] * sums[0], axis=1, keepdims=True) + jnp.sum(
        sums[1] * sums[1], axis=1, keepdims=True
    )
    renewed = accum_ref[...] + square * (1.0 / width)
    new_ref[...] = renewed
    scale = 1.0 / jnp.sqrt(renewed)
    side = side_ref[0]
    near = pl.multiple_of(side * half, 128)
    far = pl.multiple_of((1 - side) * half, 128)
    out_ref[0, :, pl.ds(near, half)] = sums[0] * scale
    out_ref[0, :, pl.ds(far, half)] = sums[1] * scale


def weight_update(side, accum, near_parts, far_parts, layer_idx, depth, whole):
    parts = len(near_parts)
    share, half = near_parts[0].shape
    tile = 32
    piece = pl.BlockSpec((tile, half), lambda i, s: (i, 0))
    single = pl.BlockSpec((tile, 1), lambda i, s: (i, 0))
    carried = [] if whole is None else [whole]
    return pl.pallas_call(
        functools.partial(step_kernel, parts),
        out_shape=[
            jax.ShapeDtypeStruct((depth, share, 2 * half), jnp.float32),
            jax.ShapeDtypeStruct((share, 1), jnp.float32),
        ],
        grid_spec=pltpu.PrefetchScalarGridSpec(
            num_scalar_prefetch=1,
            grid=(share // tile,),
            in_specs=[single] + [piece] * (2 * parts) + [pl.BlockSpec(memory_space=pl.ANY)] * len(carried),
            out_specs=[
                pl.BlockSpec((1, tile, 2 * half), lambda i, s: (layer_idx, i, 0)),
                single,
            ],
        ),
        input_output_aliases={2 + 2 * parts: 0} if carried else {},
        compiler_params=pltpu.CompilerParams(vmem_limit_bytes=32 * 1024 * 1024),
        cost_estimate=pl.CostEstimate(
            flops=8 * share * half,
            bytes_accessed=share * half * (8 + 4 * parts),
            transcendentals=0,
        ),
        name="weight_update",
    )(side, accum, *near_parts, *far_parts, *carried)


def slot_kernel(embed, per_device, table_ref, summed_ref, late_ref, out_ref, joined):
    width = late_ref.shape[2]
    for m in range(late_ref.shape[0]):
        cols = slice(m * width, (m + 1) * width)
        joined[:, cols] = summed_ref[:, cols] + late_ref[m].astype(jnp.float32)
    devices, pairs, rows, lanes = out_ref.shape
    lane = lax.broadcasted_iota(jnp.int32, (rows, lanes), 1)

    def look(slot):
        first = table_ref[slot] * embed
        start = pl.multiple_of(first // lanes * lanes, 128)
        value = joined[:, pl.ds(start, lanes)]
        return value, first - start

    def one(turn_idx, carry):
        for u, p in ((u, p) for u in range(2) for p in range(pairs)):
            device = turn_idx * 2 + u
            slot = device * per_device + 2 * p
            low, low_at = look(slot)
            high, high_at = look(slot + min(1, per_device - 1 - 2 * p))
            low = jnp.where(low_at == 0, low, pltpu.roll(low, embed, 1))
            high = jnp.where(high_at == 0, pltpu.roll(high, embed, 1), high)
            out_ref[device, p] = jnp.where(lane < embed, low, high).astype(out_ref.dtype)
        return carry

    lax.fori_loop(0, devices // 2, one, 0)


def to_slots(table_of, summed, late, embed, devices):
    rows = summed.shape[0]
    per_device = table_of.shape[0] // devices
    pairs = (per_device + 1) // 2
    return pl.pallas_call(
        functools.partial(slot_kernel, embed, per_device),
        out_shape=jax.ShapeDtypeStruct((devices, pairs, rows, 2 * embed), jnp.bfloat16),
        grid_spec=pltpu.PrefetchScalarGridSpec(
            num_scalar_prefetch=1,
            grid=(1,),
            in_specs=[
                pl.BlockSpec(summed.shape, lambda i, s: (0, 0)),
                pl.BlockSpec(late.shape, lambda i, s: (0, 0, 0)),
            ],
            out_specs=pl.BlockSpec((devices, pairs, rows, 2 * embed), lambda i, s: (0, 0, 0, 0)),
            scratch_shapes=[pltpu.VMEM(summed.shape, jnp.float32)],
        ),
        compiler_params=pltpu.CompilerParams(vmem_limit_bytes=32 * 1024 * 1024),
        cost_estimate=pl.CostEstimate(
            flops=4 * rows * summed.shape[1],
            bytes_accessed=10 * rows * summed.shape[1],
            transcendentals=0,
        ),
        name="to_slots",
    )(table_of, summed, late)


def body(
    features,
    cotangent,
    weights,
    biases,
    weight_accum,
    owner_slot,
    bag_ids,
    bag_length,
    tables,
    table_accum,
):
    depth, block_cols, full_width = weights.shape
    data_size = lax.axis_size("dp")
    model_size = lax.axis_size("mp")
    line = model_size // cores
    model_index = lax.axis_index("mp")
    data_index = lax.axis_index("dp")
    spot = model_index // cores
    core = model_index % cores
    first_core = core == 0
    rows = features.shape[0]
    members = data_size // 2
    f32, bf16 = jnp.float32, jnp.bfloat16

    def swap(value):
        return lax.ppermute(value, "mp", [(i, i ^ 1) for i in range(model_size)])

    def hop(value, right, left):
        pairs = [(z * cores, (z + 1) * cores) for z in right]
        pairs += [(z * cores + 1, (z - 1) * cores + 1) for z in left]
        return lax.ppermute(value, "mp", pairs)

    def chip_pair(value):
        other = swap(value)
        return jnp.where(
            first_core,
            jnp.concatenate([value, other], axis=1),
            jnp.concatenate([other, value], axis=1),
        )

    def selected(held, k):
        up, down = held[line - k], held[k]
        if 2 * k == line:
            return up, down
        return jnp.where(first_core, up, down), jnp.where(first_core, down, up)

    def chips(offsets):
        return jnp.stack([(spot + j) % line for j in offsets]).astype(jnp.int32)

    def by_columns(scaled, layer_idx):
        width = cores * block_cols
        held = {}

        def products(offsets, *needed):
            product = column_blocks(
                after(chips(offsets), *needed), scaled, weights, layer_idx, width
            )
            for at, j in enumerate(offsets):
                held[j] = product[at]
            return product

        first = products((1, line - 1))
        rest = lambda sent: (products((*range(2, line - 1), 0), sent),)
        return first, lambda k: selected(held, k), lambda: held[0], rest

    def by_rows(scaled, layer_idx):
        product = row_blocks_product(chips(range(line)), scaled, weights, layer_idx)
        held = [product[j] for j in range(line)]
        return product, lambda k: selected(held, k), lambda: held[0], lambda sent: ()

    def gather_and_reduce(chip, partial, axis, fill, between, complete, reduce_first):
        width = chip.shape[1]
        first, pair, own, rest = partial
        wide = lax.dynamic_update_slice_in_dim(blank((rows, full_width)), chip, spot * width, 1)
        moving = hop(chip, range(0, line - 1), range(1, line))
        moving = after(moving, first)
        inbound, ready = None, None
        if reduce_first:
            mine, theirs = pair(1)
            crossed = after(swap(theirs), *rest(theirs))
            ready = (mine.astype(f32) + crossed.astype(f32)).astype(bf16)
            moving = after(moving, ready)
        for k in range(1, line):
            passed = swap(moving)
            ahead = None
            if k + 1 < line:
                ahead = hop(moving, range(k, line - 1), range(1, line - k))
            for piece, up in ((moving, first_core), (passed, ~first_core)):
                place = jnp.where(up, spot - k, spot + k)
                here = (place >= 0) & (place < line)
                wide = lax.dynamic_update_slice_in_dim(
                    wide, jnp.where(here, piece, chip), jnp.where(here, place, spot) * width, 1
                )
            if k + 1 == line:
                inbound = after(inbound, *complete(wide))
            elif inbound is not None:
                inbound = after(inbound, *between(k, moving))
            if ready is not None:
                total, ready = ready, None
            else:
                mine, theirs = pair(k)
                crossed = swap(theirs)
                total = mine.astype(f32) + crossed.astype(f32)
                if inbound is not None:
                    total = total + inbound.astype(f32)
                total = total.astype(bf16)
            inbound = hop(total, range(k), range(line - k, line))
            if ahead is not None:
                moving = after(ahead, total, *fill(k, total, moving))

        def finish(*needed):
            last = after(inbound, *needed)
            local = own()
            part = local.shape[axis] // cores

            def portion(at):
                return lax.dynamic_slice_in_dim(local, at * part, part, axis).astype(
                    f32
                ) + lax.dynamic_slice_in_dim(last, at * part, part, axis).astype(f32)

            sent = portion(1 - core).astype(bf16)
            return portion(core) + swap(sent).astype(f32)

        return wide, finish

    def crossing(low_core, high_core):
        pairs = []
        for d in range(data_size):
            for m in range(model_size):
                target = (high_core if m % cores else low_core)(d)
                pairs.append((d * model_size + m, target * model_size + m))
        return pairs

    def cross(value, low_core, high_core):
        return lax.ppermute(value, ("dp", "mp"), crossing(low_core, high_core))

    low_flip = lambda d: d ^ 1
    top_flip = lambda d: (d + members) % data_size
    low_turn = lambda k: lambda d: (d // 2 + k) % members * 2 + d % 2
    top_turn = lambda k: lambda d: d // members * members + (d % members + k) % members
    low_bit, low_rest = data_index % 2, data_index // 2
    top_bit, top_rest = data_index // members, data_index % members

    side = core.astype(jnp.int32)
    share = block_cols // data_size
    own_low = (first_core, ~first_core)

    def row_blocks(which, flip):
        turns = jnp.arange(members, dtype=jnp.int32)
        low = (low_rest + turns) % members * 2 + (low_bit ^ flip)
        top = (top_bit ^ flip) * members + (top_rest + turns) % members
        return jnp.where(own_low[which], low, top).astype(jnp.int32)

    sent_index = jnp.concatenate([row_blocks(0, 1), row_blocks(1, 1)])
    grad_index = [
        jnp.concatenate([(side if which == 0 else 1 - side)[None], row_blocks(which, 0)])
        for which in range(2)
    ]
    flips = ((low_flip, top_flip), (top_flip, low_flip))

    def layer_neighbour(wide, *needed):
        sent = column_half(after(side[None], *needed), wide)
        near = cross(sent, *flips[0])
        return (near, swap(near)), sent

    def turned_sums(scaled, *needed):
        turned, own_sent, other_sent = turn(after(sent_index, *needed), scaled, members, share)
        return turned, cross(own_sent, *flips[0]), cross(other_sent, *flips[1])

    def half_sums(which, turned, wide, neighbours, *needed):
        pieces = half_grad(
            after(grad_index[which], *needed),
            turned[0],
            turned[1 + which],
            wide,
            neighbours[which],
        )
        arrived = [pieces[0]]
        for k in range(1, members):
            turns = (low_turn(k), top_turn(k))
            arrived.append(cross(pieces[k], *(turns if which == 0 else turns[::-1])))
        return arrived

    base_f32 = features.astype(f32)
    top_up = cotangent.astype(f32)
    none = lambda k, moving: ()

    def preact_of(wide, layer_idx):
        return forward_product(wide, weights, biases[layer_idx], layer_idx)

    chip = chip_pair(features)
    top_scaled = (after(cotangent, chip).astype(f32) * base_f32).astype(bf16)
    top_turned = []

    def fill_top(k, total, moving):
        if k == 1:
            top_turned.extend(turned_sums(top_scaled, total))
            return (top_turned[0],)
        return ()

    nears = []

    def complete_top(wide):
        near, sent = layer_neighbour(wide)
        nears.append(near)
        return (sent,)

    def complete_low(wide):
        near, sent = layer_neighbour(wide)
        nears.append(near)
        return (sent,)

    first_wide, low_up = gather_and_reduce(
        chip, by_columns(top_scaled, 1), 1, fill_top, none, complete_top, True
    )
    first_pre = preact_of(first_wide, 0)
    current = (base_f32 * first_pre + base_f32).astype(bf16)
    chip = chip_pair(current)
    low_up = top_up + low_up(chip)
    low_scaled = (after(low_up, chip) * base_f32).astype(bf16)
    low_turned, low_sums = [], []

    def fill_low(k, total, moving):
        if k == 1:
            low_turned.extend(turned_sums(low_scaled, moving))
            return (low_turned[0],)
        if k == 2:
            low_half(1, total)
        return ()

    def low_half(which, *needed):
        low_sums.append(half_sums(which, low_turned, first_wide, nears[0], *needed))
        return (low_sums[which][0],)

    def between_low(k, moving):
        return low_half(0, moving) if k == 2 else ()

    second_wide, summed = gather_and_reduce(
        chip, by_rows(low_scaled, 0), 0, fill_low, between_low, complete_low, False
    )
    second_pre = preact_of(second_wide, 1)
    late = (low_up + low_up * first_pre + top_up * second_pre).astype(bf16)
    summed = summed(late)
    late_sent = late
    late = lax.all_to_all(
        late.reshape(model_size, rows // model_size, block_cols),
        "mp",
        split_axis=0,
        concat_axis=0,
        tiled=True,
    )
    tables_all = owner_slot.shape[0]
    embed = full_width // tables_all
    table_of = (
        jnp.zeros((tables_all,), jnp.int32)
        .at[owner_slot]
        .set(jnp.arange(tables_all, dtype=jnp.int32))
    )
    slotted = to_slots(table_of, summed, late, embed, data_size * model_size)
    arrived = lax.all_to_all(slotted, ("dp", "mp"), split_axis=0, concat_axis=0, tiled=True)
    top_sums = [half_sums(which, top_turned, second_wide, nears[1], slotted) for which in range(2)]
    whole, low_accum = weight_update(
        after(side[None], late_sent), weight_accum[0][:, None], *low_sums, 0, depth, None
    )
    arrived = after(arrived, top_sums[0][0], top_sums[1][0], low_accum)

    _, batch, bag = bag_ids.shape
    vocab = tables.shape[1]
    in_bag = jnp.arange(bag, dtype=jnp.int32)[None, None, :] < bag_length[:, :, None]
    ids = jnp.where(in_bag, bag_ids, vocab).transpose(0, 2, 1).reshape(-1)
    new_tables, new_accum = embed_update(
        ids, arrived, jnp.swapaxes(tables, 1, 2), table_accum, bag, batch, learn_rate
    )
    whole, top_accum = weight_update(
        after(side[None], new_accum), weight_accum[1][:, None], *top_sums, 1, depth, whole
    )
    accums = jnp.stack([low_accum[:, 0], top_accum[:, 0]])
    return (whole, accums, jnp.swapaxes(new_tables, 1, 2), new_accum)


def solution(mesh):
    return jax.shard_map(
        body,
        mesh=mesh,
        in_specs=(
            P("dp", "mp"),
            P("dp", "mp"),
            P(None, "mp", None),
            P(None, "mp"),
            P(None, ("mp", "dp")),
            P(),
            P(("dp", "mp"), None, None),
            P(("dp", "mp"), None),
            P(("dp", "mp"), None, None),
            P(("dp", "mp"), None),
        ),
        out_specs=(
            P(None, ("mp", "dp"), None),
            P(None, ("mp", "dp")),
            P(("dp", "mp"), None, None),
            P(("dp", "mp"), None),
        ),
        check_vma=False,
    )
```
